32 devices in a mesh: groups: 1, ctx: 16 (over z, y, core), pipe: 2 (over x), dp: 1.
Axes of the slice: x: 2, y: 2, z: 4, core: 2. Of those that a mesh axis runs over, the one named last changes fastest.
Arguments:
- rows_in: bfloat16 [2, 1, 4096, 1024], P(('groups', 'pipe'), 'dp', 'ctx'), may hold values from -6 to 6
- queries: bfloat16 [2, 1, 4096, 1024], P(('groups', 'pipe'), 'dp', 'ctx'), may hold values from -6 to 6
- keys: bfloat16 [2, 1, 4096, 1024], P(('groups', 'pipe'), 'dp', 'ctx'), may hold values from -12 to 12
- strengths: float32 [2, 1, 8, 4096], P(('groups', 'pipe'), 'dp', None, 'ctx'), may hold values from 0.05 to 0.5
- gates: float32 [2, 1, 8, 4096], P(('groups', 'pipe'), 'dp', None, 'ctx'), may hold values from 0.45 to 1
- doc_ids: int32 [2, 1, 4096], P(('groups', 'pipe'), 'dp', 'ctx'), may hold values from 0 to 7, never falling along the last dimension, each value on 1 to 1024 neighbouring positions
- positives: int32 [2, 1, 8], P(('groups', 'pipe'), 'dp'), may hold values from 0 to 7, as said below
- norm_gain: float32 [2, 128], P('pipe'), may hold values from 0.5 to 1.5
Outputs:
- rows_next: bfloat16 [2, 1, 4096, 1024], P(('groups', 'pipe'), 'dp', 'ctx')
- doc_loss: float32 [2, 1, 8], P(('groups', 'pipe'), 'dp')
The draws below stay inside these ranges and needn't reach their ends.
Inputs may be any that keep to these rules, and one draw needn't show every extreme that they name: `positives`: never the document's own index dp * 8 + its document number.
All inputs are finite; a program needn't handle non-finite values.
Results may differ from the reference program's by a relative error of at most 0.008.
Values may be sent and summed in bfloat16 or wider, within the bound.
No kernel may reach another device: no remote copies, remote signals or barrier semaphores. Data moves between devices by JAX's collectives and lax.ppermute only.
A program may use at most 128 MiB of HBM per device.

```python
import math
import jax
import jax.numpy as jnp
import numpy as np
from jax import lax

HEADS = 8
DK = 128
NDOC = 8
HD = 1024
PACKED_TOKENS = 4096
MOST = 1024
CANDS = 8
N_PIPE = 2
N_DP = 1


def draw_gates(key, part):
    level_random_key, jitter_key, spike_random_key, depth_random_key, category_key = jax.random.split(key, 5)
    tensor_dimensions = (N_PIPE, N_DP, HEADS, PACKED_TOKENS)
    position = jax.random.uniform(level_random_key, (N_PIPE, N_DP, HEADS, 1))
    class_pick = jax.random.uniform(category_key, (N_PIPE, N_DP, HEADS, 1))
    middle_speed = math.log(1.0 / 92.0) + position * math.log(92.0 / 80.0)
    quick_speed = math.log(1.0 / 50.0) + position * math.log(50.0 / 30.0)
    slow_speed = math.log(1.0 / (4.0 * PACKED_TOKENS)) + position * math.log(8.0)
    decay_speed = jnp.where(class_pick < 0.25, quick_speed, jnp.where(class_pick < 0.5, middle_speed, slow_speed))
    jitter_amount = jnp.exp(jax.random.uniform(jitter_key, tensor_dimensions, minval=-0.7, maxval=0.7))
    spike_selection = jax.random.uniform(spike_random_key, tensor_dimensions) < 4.0 / PACKED_TOKENS
    spike_depth = jax.random.uniform(depth_random_key, tensor_dimensions, minval=0.5, maxval=0.8)
    forget_weight = jnp.exp(-jnp.exp(decay_speed) * jitter_amount) * jnp.where(spike_selection, spike_depth, 1.0)
    return forget_weight.astype(jnp.float32)


def draw_keys(key, part):
    shared_key, noise_key = jax.random.split(jax.random.fold_in(key, 7), 2)
    full_extents = (N_PIPE, N_DP, PACKED_TOKENS, HEADS, DK)
    noise = jax.random.normal(noise_key, full_extents)
    shared_scale = 3.0 * jnp.ones((N_PIPE, N_DP, 1, HEADS, 1), jnp.float32)
    shared = jax.random.normal(shared_key, (N_PIPE, N_DP, 1, HEADS, DK)) * shared_scale
    combined = jnp.clip(shared + noise, -12.0, 12.0).astype(jnp.float32)
    return combined.reshape(N_PIPE, N_DP, PACKED_TOKENS, HEADS * DK).astype(jnp.bfloat16)


def draw_positives(key, part):
    own = jnp.arange(N_DP, dtype=jnp.int32)[:, None] * NDOC + jnp.arange(NDOC, dtype=jnp.int32)[None, :]
    offset = jax.random.randint(key, (N_PIPE, N_DP, NDOC), 1, CANDS)
    return ((own[None] + offset) % CANDS).astype(jnp.int32)


def block_levels(stream_key, dims, cuts, low, top_value):
    loudness = 1.0
    for dim, blocks in cuts:
        steps = jax.random.uniform(jax.random.fold_in(jax.random.fold_in(stream_key, 6), dim), (blocks,), jnp.float32, low / len(cuts), top_value / len(cuts))
        loudness = loudness * jnp.repeat(jnp.exp(steps), dims[dim] // blocks).reshape((-1,) + (1,) * (len(dims) - 1 - dim))
    return loudness


def profile(amount, total, bound, lean):
    portions = [(1 << 20) // math.isqrt(rank ** lean) + 1 for rank in range(2, amount + 1)]
    surplus, counts = total - bound - (amount - 1), [1] * (amount - 1)
    while surplus > 0:
        free = [i for i in range(amount - 1) if counts[i] < bound]
        whole, remaining = sum([portions[i] for i in free]), surplus
        for i in free:
            addition = min(bound - counts[i], max(1, remaining * portions[i] // whole), surplus)
            counts[i] = counts[i] + addition
            surplus = surplus - addition
    return np.array([bound] + counts)


def ragged_sizes(stream_key, amount, total, limit, slope):
    if amount == 2:
        one = jax.random.randint(stream_key, (), max(1, total - limit), min(limit, total - 1) + 1)
        return jnp.stack([one, total - one])
    lengths = jnp.asarray(profile(amount, total, limit, slope), jnp.int32)
    twos = (amount - 1) // 2
    donor, receiver = lengths[1:1 + 2 * twos:2], lengths[2:2 + 2 * twos:2]
    slack = jnp.minimum(donor - 1, limit - receiver)
    passed = jax.random.randint(jax.random.fold_in(stream_key, 1), (twos,), 0, 1 << 20) % (slack + 1)
    lengths = lengths.at[1:1 + 2 * twos:2].set(donor - passed).at[2:2 + 2 * twos:2].set(receiver + passed)
    return lengths[jax.random.permutation(jax.random.fold_in(stream_key, 2), amount)]


def gaussian(key, shape, width, reach, cuts=(), kind=jnp.bfloat16):
    result = jax.random.normal(key, shape, jnp.float32) * width
    if len(cuts) > 0:
        result = block_levels(key, shape, cuts, -0.22, 0.18) * result
    return jnp.clip(result, min=-reach, max=reach).astype(kind)


def setup_inputs(seed: int = 0, part: int = 0) -> dict:
    key_list = jax.random.split(jax.random.key(seed), 9)
    part_splits = jax.random.split(jax.random.fold_in(key_list[8], part), 9)
    rows_in = gaussian(part_splits[0], (N_PIPE, N_DP, PACKED_TOKENS, HD), 1.0, 6.0, ((0, 2), (2, 16)))
    queries = gaussian(part_splits[1], (N_PIPE, N_DP, PACKED_TOKENS, HD), 1.0, 6.0, ((0, 2), (2, 16)))
    keys = draw_keys(jax.random.fold_in(jax.random.fold_in(key_list[8], part), 71), part)
    strengths = jnp.clip(jnp.exp(math.log(0.5) - 2.3025851 * jax.random.uniform(part_splits[3], (N_PIPE, N_DP, HEADS, PACKED_TOKENS), jnp.float32) ** block_levels(part_splits[3], (N_PIPE, N_DP, HEADS, PACKED_TOKENS), ((0, 2), (3, 16)), -0.2, 0.2)), 0.05, 0.5)
    gates = draw_gates(jax.random.fold_in(jax.random.fold_in(key_list[8], part), 71), part)
    doc_ids = jax.vmap(lambda own: jnp.searchsorted(jnp.cumsum(ragged_sizes(own, NDOC, PACKED_TOKENS, MOST, 0)), jnp.arange(PACKED_TOKENS), side="right"))(jax.random.split(part_splits[5], N_PIPE * N_DP)).reshape((N_PIPE, N_DP, PACKED_TOKENS)).astype(jnp.int32)
    positives = draw_positives(jax.random.fold_in(jax.random.fold_in(key_list[8], part), 71), part)
    norm_gain = jnp.clip(1.0 + 0.1 * jax.random.normal(key_list[7], (N_PIPE, DK), jnp.float32), 0.5, 1.5)
    return dict(rows_in=rows_in, queries=queries, keys=keys, strengths=strengths, gates=gates, doc_ids=doc_ids, positives=positives, norm_gain=norm_gain)


def unit_rows(x):
    return x * lax.rsqrt(lax.optimization_barrier(jnp.sum(x * x, axis=-1, keepdims=True)) + 1e-06)

def reference(rows_in, queries, keys, strengths, gates, doc_ids, positives, norm_gain):
    hi = lax.Precision.HIGHEST
    npipe, ndp, seq = (rows_in.shape[0], rows_in.shape[1], rows_in.shape[2])
    values = rows_in.astype(jnp.float32).reshape(npipe, ndp, seq, HEADS, DK)
    qn = unit_rows(queries.astype(jnp.float32).reshape(npipe, ndp, seq, HEADS, DK))
    kn = unit_rows(keys.astype(jnp.float32).reshape(npipe, ndp, seq, HEADS, DK))
    before = jnp.concatenate([doc_ids[:, :, :1], doc_ids[:, :, :-1]], axis=2)
    reset = (doc_ids != before).astype(jnp.float32)
    decay = gates * (1.0 - reset)[:, :, None, :]

    def advance(state, inputs):
        key_t, value_t, query_t, decay_t, beta_t = inputs
        proj = jnp.einsum('pbhk,pbhkv->pbhv', key_t, state, precision=hi)
        state = decay_t[..., None, None] * (state - beta_t[..., None, None] * key_t[..., :, None] * proj[..., None, :])
        state = state + beta_t[..., None, None] * key_t[..., :, None] * value_t[..., None, :]
        out = jnp.einsum('pbhk,pbhkv->pbhv', query_t, state, precision=hi)
        return (state, out)
    start = jnp.zeros((npipe, ndp, HEADS, DK, DK), jnp.float32)
    inputs = (jnp.moveaxis(kn, 2, 0), jnp.moveaxis(values, 2, 0), jnp.moveaxis(qn, 2, 0), jnp.moveaxis(decay, 3, 0), jnp.moveaxis(strengths, 3, 0))
    _, outs = lax.scan(advance, start, inputs)
    outs = jnp.moveaxis(outs, 0, 2)
    scale = lax.rsqrt(lax.optimization_barrier(jnp.mean(outs * outs, axis=-1, keepdims=True)) + 1e-06)
    normed = outs * scale * norm_gain[:, None, None, None, :]
    rows_out = (values + normed).reshape(npipe, ndp, seq, HEADS * DK).astype(jnp.bfloat16)
    rows_next = jnp.roll(rows_out, 1, axis=0)
    ndoc = positives.shape[2]
    onehot = (jnp.arange(ndoc, dtype=jnp.int32)[None, None, :, None] == doc_ids[:, :, None, :]).astype(jnp.float32)
    pooled = jnp.einsum('pbjs,pbsd->pbjd', onehot, rows_out.astype(jnp.float32), precision=hi)
    emb = unit_rows(pooled)
    cands = emb.reshape(npipe, ndp * ndoc, HEADS * DK)
    scores = jnp.einsum('pbjd,pcd->pbjc', emb, cands, precision=hi) / 0.05
    own = jnp.arange(ndp, dtype=jnp.int32)[:, None] * ndoc + jnp.arange(ndoc, dtype=jnp.int32)[None, :]
    cidx = jnp.arange(ndp * ndoc, dtype=jnp.int32)
    others = cidx[None, None, None, :] != own[None, :, :, None]
    total = lax.optimization_barrier(jnp.sum(jnp.where(others, jnp.exp(scores), 0.0), axis=-1))
    picked = lax.optimization_barrier(jnp.sum(jnp.where(cidx[None, None, None, :] == positives[..., None], scores, 0.0), axis=-1))
    doc_loss = jnp.log(total) - picked
    return (rows_next, doc_loss)
```

```python
import functools

import jax
import jax.numpy as jnp
from jax import lax
from jax.experimental import pallas as pl
from jax.experimental.pallas import tpu as pltpu
from jax.sharding import PartitionSpec as P

F32, BF16 = jnp.float32, jnp.bfloat16
HIGHEST = lax.Precision.HIGHEST
NEG = -1e30
SUB = 128
META = 16

NN = (((1,), (0,)), ((), ()))
NT = (((1,), (1,)), ((), ()))
TN = (((0,), (0,)), ((), ()))


def dot(a, b, dims=NN, precision=None):
    return lax.dot_general(a, b, dims, precision=precision, preferred_element_type=F32)


def dot1(a, b, dims=NN):
    return dot(a.astype(BF16), b.astype(BF16), dims)


def split(x):
    high = x.astype(BF16)
    return high, (x - high.astype(F32)).astype(BF16)


def dot3(a, b, dims=NN):
    (ah, al), (bh, bl) = split(a), split(b)
    return dot(ah, bh, dims) + (dot(al, bh, dims) + dot(ah, bl, dims))


def unit(x):
    return x * lax.rsqrt(jnp.sum(x * x, axis=-1, keepdims=True) + 1e-06)


def iotas():
    shape = (SUB, SUB)
    return lax.broadcasted_iota(jnp.int32, shape, 0), lax.broadcasted_iota(jnp.int32, shape, 1)


def per_token(rows, heads, subs):
    return jnp.concatenate([rows[:, j * SUB : (j + 1) * SUB] for j in range(subs)], axis=0)


class Decay:
    def __init__(self, gates, ids, heads, subs):
        r, c = iotas()
        upto = (c <= r).astype(F32)
        logs = per_token(jnp.log(gates), heads, subs)
        self.row = dot(logs, upto, NT, HIGHEST)
        self.col = dot(upto, logs, NT, HIGHEST)
        ids = ids.astype(F32)
        eye = (r == c).astype(F32)
        self.id_row = [ids[:, j * SUB : (j + 1) * SUB] for j in range(subs)]
        stacked = jnp.concatenate([jnp.broadcast_to(x, (8, SUB)) for x in self.id_row], axis=0)
        turned = dot1(eye, stacked, NT)
        self.id_col = [turned[:, 8 * j : 8 * j + 1] for j in range(subs)]
        self.heads, self.r, self.c, self.eye = heads, r, c, eye

    def rows(self, h, j):
        i = j * self.heads + h
        return self.row[i : i + 1, :]

    def cols(self, h, j):
        i = j * self.heads + h
        return self.col[:, i : i + 1]

    def inner(self, h, j):
        keep = (self.id_col[j] == self.id_row[j]) & (self.r >= self.c)
        return jnp.exp(jnp.where(keep, self.cols(h, j) - self.rows(h, j), NEG))

    def entry(self, j):
        return self.id_row[0][:, :1] if j == 0 else self.id_row[j - 1][:, SUB - 1 :]

    def lead(self, h, j):
        return jnp.where(self.id_col[j] == self.entry(j), jnp.exp(self.cols(h, j)), 0.0)

    def lead_end(self, h, j):
        last = self.rows(h, j)[:, SUB - 1 :]
        return jnp.where(self.id_row[j][:, SUB - 1 :] == self.entry(j), jnp.exp(last), 0.0)

    def tail(self, h, j):
        keep = self.id_col[j] == self.id_row[j][:, SUB - 1 :]
        return jnp.exp(jnp.where(keep, self.rows(h, j)[:, SUB - 1 :] - self.cols(h, j), NEG))


def block(ref, h, j):
    return ref[j * SUB : (j + 1) * SUB, h * SUB : (h + 1) * SUB]


def chunk_kernel(
    heads, subs, core_ref, k_ref, v_ref, beta_ref, gates_ref, ids_ref,
    send_ref, keep_ref, wv_ref, yy_ref, p0_ref, u0_ref,
):
    decay = Decay(gates_ref[...], ids_ref[...], heads, subs)
    r, c, eye = decay.r, decay.c, decay.eye
    beta = dot(eye, per_token(beta_ref[...], heads, subs), NT, HIGHEST)
    chains = [(h, j) for j in range(subs) for h in range(heads)]
    kn, low, inv, bt = {}, {}, {}, {}
    for h, j in chains:
        i = j * heads + h
        kn[h, j] = unit(block(k_ref, h, j).astype(F32))
        bt[h, j] = beta[:, i : i + 1]
    for h, j in chains:
        gram = dot1(kn[h, j], kn[h, j], NT)
        full = jnp.where(r > c, bt[h, j] * decay.inner(h, j) * gram, 0.0)
        near = ((r // 2) == (c // 2)) & (r > c)
        inv[h, j] = eye - jnp.where(near, full, 0.0)
        low[h, j] = full.astype(BF16)
    size = 2
    while size < SUB:
        pick = (((r // size) % 2 == 1) & ((c // size) == (r // size) - 1)).astype(BF16)
        half = {}
        for key in chains:
            half[key] = dot1(inv[key], low[key] * pick)
        for key in chains:
            inv[key] = inv[key] - dot1(half[key], inv[key])
        size *= 2
    wv, yy, pp, uu = {}, {}, {}, {}
    for h, j in chains:
        lead = bt[h, j] * decay.lead(h, j)
        xh, xl = split(inv[h, j])
        rh, rl = split(bt[h, j] * block(v_ref, h, j).astype(F32))
        wv[h, j] = dot(xh, rh) + (dot(xl, rh) + dot(xh, rl))
        yy[h, j] = dot(xh, (lead * kn[h, j]).astype(BF16)).astype(BF16)
        wv_ref[j * SUB : (j + 1) * SUB, h * SUB : (h + 1) * SUB] = wv[h, j]
        yy_ref[j * SUB : (j + 1) * SUB, h * SUB : (h + 1) * SUB] = yy[h, j]
    for h, j in chains:
        dh, dl = split(decay.tail(h, j) * kn[h, j])
        wh, wl = split(wv[h, j])
        pp[h, j] = decay.lead_end(h, j) * eye - dot(dh, yy[h, j], TN)
        uu[h, j] = dot(dh, wh, TN) + (dot(dl, wh, TN) + dot(dh, wl, TN))
    for h in range(heads):
        p0_ref[h * SUB : (h + 1) * SUB, :] = pp[h, 0].astype(BF16)
        u0_ref[h * SUB : (h + 1) * SUB, :] = uu[h, 0].astype(BF16)
    for j in range(1, subs):
        for h in range(heads):
            step = pp[h, j].astype(BF16)
            uu[h, 0] = uu[h, j] + dot1(step, uu[h, 0])
            pp[h, 0] = dot1(step, pp[h, 0])
    half_heads = heads // 2
    first = core_ref[0] == 0
    for h in range(half_heads):
        for base, part in ((0, pp), (half_heads, uu)):
            lo, hi = part[h, 0].astype(BF16), part[half_heads + h, 0].astype(BF16)
            at = slice((base + h) * SUB, (base + h + 1) * SUB)
            send_ref[at, :] = jnp.where(first, hi, lo)
            keep_ref[at, :] = jnp.where(first, lo, hi)
    start = decay.id_row[0][:, :1]
    end = decay.id_row[-1][:, SUB - 1 :]
    which = lax.broadcasted_iota(jnp.int32, (META, SUB), 0) < META // 2
    meta = jnp.where(which, end, start).astype(BF16)
    send_ref[heads * SUB :, :] = meta
    keep_ref[heads * SUB :, :] = meta


def query_kernel(
    heads, subs, q_ref, k_ref, gates_ref, ids_ref, wv_ref, yy_ref, p0_ref, u0_ref, local_ref, reach_ref
):
    decay = Decay(gates_ref[...], ids_ref[...], heads, subs)
    chains = [(h, j) for j in range(subs) for h in range(heads)]
    qn, attend, reach, local = {}, {}, {}, {}
    for h, j in chains:
        qn[h, j] = unit(block(q_ref, h, j).astype(F32))
        kn = unit(block(k_ref, h, j).astype(F32))
        attend[h, j] = decay.inner(h, j) * dot3(qn[h, j], kn, NT)
    for h, j in chains:
        ah, al = split(attend[h, j])
        wh, wl = split(block(wv_ref, h, j))
        reach[h, j] = decay.lead(h, j) * qn[h, j] - dot(ah, block(yy_ref, h, j))
        local[h, j] = dot(ah, wh) + (dot(al, wh) + dot(ah, wl))
    for h, j in chains:
        if j > 0:
            rb = reach[h, j].astype(BF16)
            at = slice(h * SUB, (h + 1) * SUB)
            local[h, j] = local[h, j] + dot(rb, u0_ref[at, :])
            reach[h, j] = dot(rb, p0_ref[at, :])
        local_ref[j * SUB : (j + 1) * SUB, h * SUB : (h + 1) * SUB] = local[h, j]
        reach_ref[j * SUB : (j + 1) * SUB, h * SUB : (h + 1) * SUB] = reach[h, j].astype(BF16)


def ends(ref, rows):
    meta = ref[rows : rows + META, :].astype(F32)
    return meta[META // 2 : META // 2 + 1, :], meta[:1, :]


def pair_kernel(heads, core_ref, keep_ref, got_ref, full_ref, tail_ref):
    half = heads // 2
    first = core_ref[0] == 0
    own, other = ends(keep_ref, heads * SUB), ends(got_ref, heads * SUB)
    early = [jnp.where(first, a, b) for a, b in zip(own, other)]
    late = [jnp.where(first, b, a) for a, b in zip(own, other)]
    joined = (early[1] == late[0]).astype(F32)
    for h in range(half):
        at, up = slice(h * SUB, (h + 1) * SUB), slice((half + h) * SUB, (half + h + 1) * SUB)
        p1 = jnp.where(first, keep_ref[at, :], got_ref[at, :])
        p2 = jnp.where(first, got_ref[at, :], keep_ref[at, :])
        u1 = jnp.where(first, keep_ref[up, :], got_ref[up, :])
        u2 = jnp.where(first, got_ref[up, :], keep_ref[up, :])
        full_ref[at, :] = (joined * dot(p2, p1)).astype(BF16)
        state = (u2.astype(F32) + joined * dot(p2, u1)).astype(BF16)
        full_ref[up, :] = state
        tail_ref[at, :] = state
    which = lax.broadcasted_iota(jnp.int32, (META, SUB), 0) < META // 2
    meta = jnp.where(which, late[1], early[0]).astype(BF16)
    full_ref[heads * SUB :, :] = meta
    tail_ref[half * SUB :, :] = meta


def enter_kernel(heads, reach, core_ref, keep_ref, got_ref, *refs):
    chips, (send_ref, mine_ref) = refs[:reach], refs[reach:]
    half = heads // 2
    first = core_ref[0] == 0
    own, other = ends(keep_ref, heads * SUB), ends(got_ref, heads * SUB)
    early = [jnp.where(first, a, b) for a, b in zip(own, other)]
    late = [jnp.where(first, b, a) for a, b in zip(own, other)]
    marks = [(early[0], None)]
    for d, ref in enumerate(chips):
        marks.append(ends(ref, (heads if d < reach - 1 else half) * SUB))
    links = [(marks[d][0] == marks[d + 1][1]).astype(F32) for d in range(reach)]
    joined = (early[1] == late[0]).astype(F32)
    for h in range(half):
        at, up = slice(h * SUB, (h + 1) * SUB), slice((half + h) * SUB, (half + h + 1) * SUB)
        state = chips[-1][at, :].astype(F32)
        for d in range(reach - 2, -1, -1):
            state = chips[d][up, :].astype(F32) + links[d + 1] * dot1(chips[d][at, :], state)
        state = (links[0] * state).astype(BF16)
        p1 = jnp.where(first, keep_ref[at, :], got_ref[at, :])
        u1 = jnp.where(first, keep_ref[up, :], got_ref[up, :])
        middle = (joined * (u1.astype(F32) + dot(p1, state))).astype(BF16)
        send_ref[at, :] = jnp.where(first, middle, state)
        mine_ref[at, :] = jnp.where(first, state, middle)


def rows_kernel(
    heads, ndoc, copies, core_ref, mine_ref, got_ref, local_ref, reach_ref, v_ref, gain_ref, ids_ref,
    out_ref, pooled_ref,
):
    half = heads // 2
    first = core_ref[0] == 0
    length = v_ref.shape[0]
    docs = lax.broadcasted_iota(jnp.int32, (ndoc, length), 0)
    onehot = (docs == ids_ref[...]).astype(F32).astype(BF16)
    gain = gain_ref[...]
    for h in range(heads):
        at = slice((h % half) * SUB, (h % half + 1) * SUB)
        near, far = (mine_ref, got_ref) if h < half else (got_ref, mine_ref)
        state = jnp.where(first, near[at, :], far[at, :])
        cols = slice(h * SUB, (h + 1) * SUB)
        o = local_ref[:, cols] + dot(reach_ref[:, cols], state)
        scale = lax.rsqrt(jnp.sum(o * o, axis=-1, keepdims=True) * (1.0 / SUB) + 1e-06)
        out = (v_ref[:, cols].astype(F32) + o * scale * gain).astype(BF16)
        out_ref[:, cols] = out
        pooled = dot(onehot, out).astype(BF16)
        for i in range(copies):
            pooled_ref[i, :, cols] = pooled


def score(emb, cands, own, pos):
    scores = dot(cands, emb, NT, HIGHEST) / 0.05
    cidx = lax.broadcasted_iota(jnp.int32, scores.shape, 0)
    didx = lax.broadcasted_iota(jnp.int32, scores.shape, 1)
    total = jnp.sum(jnp.where(cidx != own + didx, jnp.exp(scores), 0.0), axis=0, keepdims=True)
    picked = jnp.sum(jnp.where(cidx == pos, scores, 0.0), axis=0, keepdims=True)
    return jnp.log(total) - picked


def loss_kernel(parts_ref, pos_ref, loss_ref):
    emb = unit(jnp.sum(parts_ref[...].astype(F32), axis=0))
    loss_ref[...] = score(emb, emb, 0, pos_ref[...])


def call(body, outs, name, flops=0, scalars=0, n_in=0):
    vmem = pl.BlockSpec(memory_space=pltpu.VMEM)
    smem = pl.BlockSpec(memory_space=pltpu.SMEM)
    return pl.pallas_call(
        body,
        out_shape=[jax.ShapeDtypeStruct(s, d) for s, d in outs],
        in_specs=[smem] * scalars + [vmem] * n_in,
        out_specs=[vmem] * len(outs),
        compiler_params=pltpu.CompilerParams(vmem_limit_bytes=40 << 20),
        cost_estimate=pl.CostEstimate(flops=flops, bytes_accessed=4 << 20, transcendentals=0),
        name=name,
    )


def on_device(rows_in, queries, keys, strengths, gates, doc_ids, positives, norm_gain):
    length, width = rows_in.shape[2], rows_in.shape[3]
    heads, ndoc = strengths.shape[2], positives.shape[2]
    subs = length // SUB
    half = heads // 2
    size, pipes, replicas = (lax.axis_size(x) for x in ("ctx", "pipe", "dp"))
    chips = size // 2
    reach = chips // 4
    v, q, k = rows_in[0, 0], queries[0, 0], keys[0, 0]
    beta, gate, ids = strengths[0, 0], gates[0, 0], doc_ids[0]
    core = (lax.axis_index("ctx") % 2).astype(jnp.int32).reshape(1)

    def swapped(x):
        return lax.ppermute(x, "ctx", [(i, i ^ 1) for i in range(size)])

    def from_behind(x, d):
        return lax.ppermute(x, "ctx", [(i, i + 2 * d) for i in range(size - 2 * d)])

    big = (heads * SUB + META, SUB)
    send, keep, wv, yy, p0, u0 = call(
        functools.partial(chunk_kernel, heads, subs),
        [(big, BF16), (big, BF16), ((length, width), F32), ((length, width), BF16)]
        + [((heads * SUB, SUB), BF16)] * 2,
        "chunks", scalars=1, n_in=5, flops=1 << 31,
    )(core, k, v, beta, gate, ids)
    got = swapped(send)
    full, tail = call(
        functools.partial(pair_kernel, heads),
        [(big, BF16), ((half * SUB + META, SUB), BF16)],
        "pair", scalars=1, n_in=2, flops=1 << 25,
    )(core, keep, got)
    arrived = [from_behind(full, d) for d in range(1, reach)] + [from_behind(tail, reach)]
    local, reached = call(
        functools.partial(query_kernel, heads, subs),
        [((length, width), F32), ((length, width), BF16)],
        "queries", n_in=8, flops=1 << 31,
    )(q, k, gate, ids, wv, yy, p0, u0)
    give, mine = call(
        functools.partial(enter_kernel, heads, reach),
        [((half * SUB, SUB), BF16)] * 2,
        "enter", scalars=1, n_in=2 + reach, flops=1 << 25,
    )(core, keep, got, *arrived)
    theirs = swapped(give)
    rows_out, pooled = call(
        functools.partial(rows_kernel, heads, ndoc, size),
        [((length, width), BF16), ((size, ndoc, width), BF16)],
        "rows", scalars=1, n_in=7, flops=1 << 27,
    )(core, mine, theirs, local, reached, v, norm_gain, ids)
    passed = lax.ppermute(rows_out, "pipe", [(i, (i + 1) % pipes) for i in range(pipes)])
    parts = lax.all_to_all(pooled, "ctx", 0, 0)
    pos = positives[0]
    if replicas == 1:
        (loss,) = call(loss_kernel, [((1, ndoc), F32)], "loss", n_in=2)(parts, pos)
    else:
        mine = unit(jnp.sum(parts.astype(F32), axis=0))
        cands = lax.all_gather(mine.astype(BF16), "dp", axis=0, tiled=True).astype(F32)
        loss = score(mine, cands, lax.axis_index("dp") * ndoc, pos)
    return (passed.reshape(1, 1, length, width), loss.reshape(1, 1, ndoc))


def solution(mesh):
    rows = P(("groups", "pipe"), "dp", "ctx", None)
    tokens = P(("groups", "pipe"), "dp", None, "ctx")
    docs = P(("groups", "pipe"), "dp", None)
    in_specs = (
        rows, rows, rows, tokens, tokens, P(("groups", "pipe"), "dp", "ctx"), docs, P("pipe", None)
    )
    return jax.shard_map(
        on_device, mesh=mesh, in_specs=in_specs, out_specs=(rows, docs), check_vma=False
    )
```

```python
import functools

import jax
import jax.numpy as jnp
from jax import lax
from jax.experimental import pallas as pl
from jax.experimental.pallas import tpu as pltpu
from jax.sharding import PartitionSpec as P

F32, BF16 = jnp.float32, jnp.bfloat16
HIGHEST = lax.Precision.HIGHEST
NEG = -1e30
SUB = 128
META = 16

NN = (((1,), (0,)), ((), ()))
NT = (((1,), (1,)), ((), ()))
TN = (((0,), (0,)), ((), ()))


def dot(a, b, dims=NN, precision=None):
    return lax.dot_general(a, b, dims, precision=precision, preferred_element_type=F32)


def dot1(a, b, dims=NN):
    return dot(a.astype(BF16), b.astype(BF16), dims)


def split(x):
    high = x.astype(BF16)
    return high, (x - high.astype(F32)).astype(BF16)


def dot3(a, b, dims=NN):
    (ah, al), (bh, bl) = split(a), split(b)
    return dot(ah, bh, dims) + (dot(al, bh, dims) + dot(ah, bl, dims))


def unit(x):
    return x * lax.rsqrt(jnp.sum(x * x, axis=-1, keepdims=True) + 1e-06)


def iotas():
    shape = (SUB, SUB)
    return lax.broadcasted_iota(jnp.int32, shape, 0), lax.broadcasted_iota(jnp.int32, shape, 1)


def per_token(rows, heads, subs):
    return jnp.concatenate([rows[:, j * SUB : (j + 1) * SUB] for j in range(subs)], axis=0)


class Decay:
    def __init__(self, gates, ids, heads, subs):
        r, c = iotas()
        upto = (c <= r).astype(F32)
        logs = per_token(jnp.log(gates), heads, subs)
        self.row = dot(logs, upto, NT, HIGHEST)
        self.col = dot(upto, logs, NT, HIGHEST)
        ids = ids.astype(F32)
        eye = (r == c).astype(F32)
        self.id_row = [ids[:, j * SUB : (j + 1) * SUB] for j in range(subs)]
        stacked = jnp.concatenate([jnp.broadcast_to(x, (8, SUB)) for x in self.id_row], axis=0)
        turned = dot1(eye, stacked, NT)
        self.id_col = [turned[:, 8 * j : 8 * j + 1] for j in range(subs)]
        self.heads, self.r, self.c, self.eye = heads, r, c, eye

    def rows(self, h, j):
        i = j * self.heads + h
        return self.row[i : i + 1, :]

    def cols(self, h, j):
        i = j * self.heads + h
        return self.col[:, i : i + 1]

    def inner(self, h, j):
        keep = (self.id_col[j] == self.id_row[j]) & (self.r >= self.c)
        return jnp.exp(jnp.where(keep, self.cols(h, j) - self.rows(h, j), NEG))

    def entry(self, j):
        return self.id_row[0][:, :1] if j == 0 else self.id_row[j - 1][:, SUB - 1 :]

    def lead(self, h, j):
        return jnp.where(self.id_col[j] == self.entry(j), jnp.exp(self.cols(h, j)), 0.0)

    def lead_end(self, h, j):
        last = self.rows(h, j)[:, SUB - 1 :]
        return jnp.where(self.id_row[j][:, SUB - 1 :] == self.entry(j), jnp.exp(last), 0.0)

    def tail(self, h, j):
        keep = self.id_col[j] == self.id_row[j][:, SUB - 1 :]
        return jnp.exp(jnp.where(keep, self.rows(h, j)[:, SUB - 1 :] - self.cols(h, j), NEG))


def block(ref, h, j):
    return ref[j * SUB : (j + 1) * SUB, h * SUB : (h + 1) * SUB]


def chunk_kernel(
    heads, subs, core_ref, k_hbm, v_hbm, beta_hbm, gates_hbm, ids_hbm,
    send_ref, keep_ref, wv_ref, yy_ref, p0_ref, u0_ref, k_ref, v_ref, gates_ref, ids_ref,
    beta_ref, sems,
):
    small = [(gates_hbm, gates_ref), (ids_hbm, ids_ref), (beta_hbm, beta_ref)]
    parts = [pl.ds(j * SUB, SUB) for j in range(subs)]
    large = [(x.at[p, :], y.at[p, :]) for x, y in ((k_hbm, k_ref), (v_hbm, v_ref)) for p in parts]
    copies = [pltpu.make_async_copy(x, y, sems.at[i]) for i, (x, y) in enumerate(small + large)]
    for copy in copies:
        copy.start()
    for copy in copies[:3]:
        copy.wait()
    decay = Decay(gates_ref[...], ids_ref[...], heads, subs)
    r, c, eye = decay.r, decay.c, decay.eye
    brow = per_token(beta_ref[...], heads, subs)
    beta = dot(eye, brow, NT, HIGHEST)
    chains = [(h, j) for j in range(subs) for h in range(heads)]
    kn, low, inv = {}, {}, {}
    for h, j in chains:
        if h == 0:
            copies[3 + j].wait()
        kn[h, j] = unit(block(k_ref, h, j).astype(F32))
    near = ((r // 2) == (c // 2)) & (r > c)
    for h, j in chains:
        i = j * heads + h
        gram = dot1(kn[h, j], kn[h, j], NT)
        full = jnp.where(r > c, beta[:, i : i + 1] * decay.inner(h, j) * gram, 0.0)
        inv[h, j] = eye - jnp.where(near, full, 0.0)
        low[h, j] = full.astype(BF16)
    size = 2
    while size < SUB:
        pick = (((r // size) % 2 == 1) & ((c // size) == (r // size) - 1)).astype(BF16)
        odd = range(size, SUB, 2 * size)
        half, rows = {}, {}
        for key in chains:
            rows[key] = inv[key]
            if size >= 8:
                rows[key] = jnp.concatenate([inv[key][o : o + size] for o in odd], axis=0)
            half[key] = dot1(rows[key], low[key] * pick)
        for key in chains:
            new = rows[key] - dot1(half[key], inv[key])
            if size >= 8:
                parts = []
                for n, o in enumerate(odd):
                    parts += [inv[key][o - size : o], new[n * size : (n + 1) * size]]
                new = jnp.concatenate(parts, axis=0)
            inv[key] = new
        size *= 2
    for copy in copies[3 + subs :]:
        copy.wait()
    wv, yy, pp, uu = {}, {}, {}, {}
    for h, j in chains:
        i = j * heads + h
        xh, xl = split(inv[h, j] * brow[i : i + 1, :])
        both = jnp.concatenate([block(v_ref, h, j), (decay.lead(h, j) * kn[h, j]).astype(BF16)], axis=1)
        got = dot(xh, both)
        wv[h, j] = got[:, :SUB] + dot(xl, both[:, :SUB])
        yy[h, j] = got[:, SUB:].astype(BF16)
        wv_ref[j * SUB : (j + 1) * SUB, h * SUB : (h + 1) * SUB] = wv[h, j]
        yy_ref[j * SUB : (j + 1) * SUB, h * SUB : (h + 1) * SUB] = yy[h, j]
    for h, j in chains:
        dh, dl = split(decay.tail(h, j) * kn[h, j])
        wh, wl = split(wv[h, j])
        got = dot(dh, jnp.concatenate([wh, yy[h, j]], axis=1), TN)
        pp[h, j] = decay.lead_end(h, j) * eye - got[:, SUB:]
        uu[h, j] = got[:, :SUB] + (dot(dl, wh, TN) + dot(dh, wl, TN))
    for h in range(heads):
        p0_ref[h * SUB : (h + 1) * SUB, :] = pp[h, 0].astype(BF16)
        u0_ref[h * SUB : (h + 1) * SUB, :] = uu[h, 0].astype(BF16)
    for j in range(1, subs):
        for h in range(heads):
            step = pp[h, j].astype(BF16)
            uu[h, 0] = uu[h, j] + dot1(step, uu[h, 0])
            pp[h, 0] = dot1(step, pp[h, 0])
    half_heads = heads // 2
    first = core_ref[0] == 0
    for h in range(half_heads):
        for base, part in ((0, pp), (half_heads, uu)):
            lo, hi = part[h, 0].astype(BF16), part[half_heads + h, 0].astype(BF16)
            at = slice((base + h) * SUB, (base + h + 1) * SUB)
            send_ref[at, :] = jnp.where(first, hi, lo)
            keep_ref[at, :] = jnp.where(first, lo, hi)
    start = decay.id_row[0][:, :1]
    end = decay.id_row[-1][:, SUB - 1 :]
    which = lax.broadcasted_iota(jnp.int32, (META, SUB), 0) < META // 2
    meta = jnp.where(which, end, start).astype(BF16)
    send_ref[heads * SUB :, :] = meta
    keep_ref[heads * SUB :, :] = meta


def query_kernel(
    heads, subs, q_ref, k_ref, gates_ref, ids_ref, wv_ref, yy_ref, p0_ref, u0_ref,
    gain_in, pos_in, local_ref, reach_ref, gain_ref, pos_ref,
):
    gain_ref[...] = gain_in[...]
    pos_ref[...] = pos_in[...]
    decay = Decay(gates_ref[...], ids_ref[...], heads, subs)
    chains = [(h, j) for j in range(subs) for h in range(heads)]
    qn, attend, reach, local = {}, {}, {}, {}
    for h, j in chains:
        qn[h, j] = unit(block(q_ref, h, j).astype(F32))
        kn = unit(block(k_ref, h, j).astype(F32))
        attend[h, j] = decay.inner(h, j) * dot3(qn[h, j], kn, NT)
    for h, j in chains:
        ah, al = split(attend[h, j])
        wh, wl = split(block(wv_ref, h, j))
        reach[h, j] = decay.lead(h, j) * qn[h, j] - dot(ah, block(yy_ref, h, j))
        local[h, j] = dot(ah, wh) + (dot(al, wh) + dot(ah, wl))
    for h, j in chains:
        if j > 0:
            rb = reach[h, j].astype(BF16)
            at = slice(h * SUB, (h + 1) * SUB)
            local[h, j] = local[h, j] + dot(rb, u0_ref[at, :])
            reach[h, j] = dot(rb, p0_ref[at, :])
        local_ref[j * SUB : (j + 1) * SUB, h * SUB : (h + 1) * SUB] = local[h, j]
        reach_ref[j * SUB : (j + 1) * SUB, h * SUB : (h + 1) * SUB] = reach[h, j].astype(BF16)


def ends(ref, rows):
    meta = ref[rows : rows + META, :].astype(F32)
    return meta[META // 2 : META // 2 + 1, :], meta[:1, :]


def pair_kernel(heads, core_ref, keep_ref, got_ref, full_ref, tail_ref):
    half = heads // 2
    first = core_ref[0] == 0
    own, other = ends(keep_ref, heads * SUB), ends(got_ref, heads * SUB)
    early = [jnp.where(first, a, b) for a, b in zip(own, other)]
    late = [jnp.where(first, b, a) for a, b in zip(own, other)]
    joined = (early[1] == late[0]).astype(F32)
    for h in range(half):
        at, up = slice(h * SUB, (h + 1) * SUB), slice((half + h) * SUB, (half + h + 1) * SUB)
        p1 = jnp.where(first, keep_ref[at, :], got_ref[at, :])
        p2 = jnp.where(first, got_ref[at, :], keep_ref[at, :])
        u1 = jnp.where(first, keep_ref[up, :], got_ref[up, :])
        u2 = jnp.where(first, got_ref[up, :], keep_ref[up, :])
        full_ref[at, :] = (joined * dot(p2, p1)).astype(BF16)
        state = (u2.astype(F32) + joined * dot(p2, u1)).astype(BF16)
        full_ref[up, :] = state
        tail_ref[at, :] = state
    which = lax.broadcasted_iota(jnp.int32, (META, SUB), 0) < META // 2
    meta = jnp.where(which, late[1], early[0]).astype(BF16)
    full_ref[heads * SUB :, :] = meta
    tail_ref[half * SUB :, :] = meta


def enter_kernel(heads, reach, core_ref, keep_ref, got_ref, *refs):
    chips, (send_ref, mine_ref) = refs[:reach], refs[reach:]
    half = heads // 2
    first = core_ref[0] == 0
    own, other = ends(keep_ref, heads * SUB), ends(got_ref, heads * SUB)
    early = [jnp.where(first, a, b) for a, b in zip(own, other)]
    late = [jnp.where(first, b, a) for a, b in zip(own, other)]
    marks = [(early[0], None)]
    for d, ref in enumerate(chips):
        marks.append(ends(ref, (heads if d < reach - 1 else half) * SUB))
    links = [(marks[d][0] == marks[d + 1][1]).astype(F32) for d in range(reach)]
    joined = (early[1] == late[0]).astype(F32)
    for h in range(half):
        at, up = slice(h * SUB, (h + 1) * SUB), slice((half + h) * SUB, (half + h + 1) * SUB)
        state = chips[-1][at, :].astype(F32)
        for d in range(reach - 2, -1, -1):
            state = chips[d][up, :].astype(F32) + links[d + 1] * dot1(chips[d][at, :], state)
        state = (links[0] * state).astype(BF16)
        p1 = jnp.where(first, keep_ref[at, :], got_ref[at, :])
        u1 = jnp.where(first, keep_ref[up, :], got_ref[up, :])
        middle = (joined * (u1.astype(F32) + dot(p1, state))).astype(BF16)
        send_ref[at, :] = jnp.where(first, middle, state)
        mine_ref[at, :] = jnp.where(first, state, middle)


def rows_kernel(
    heads, ndoc, copies, own, core_ref, state_ref, local_ref, reach_ref, v_ref, gain_ref, ids_ref, *refs
):
    out_ref, pooled_ref = refs[-2:]
    half = heads // 2
    group = core_ref[0] if own else 1 - core_ref[0]
    docs = lax.broadcasted_iota(jnp.int32, (ndoc, v_ref.shape[0]), 0)
    onehot = (docs == ids_ref[...]).astype(F32).astype(BF16)
    gain = gain_ref[...]
    for h in range(half):
        cols = pl.ds(pl.multiple_of((group * half + h) * SUB, SUB), SUB)
        o = local_ref[:, cols] + dot(reach_ref[:, cols], state_ref[h * SUB : (h + 1) * SUB, :])
        scale = lax.rsqrt(jnp.sum(o * o, axis=-1, keepdims=True) * (1.0 / SUB) + 1e-06)
        out = (v_ref[:, cols].astype(F32) + o * scale * gain).astype(BF16)
        out_ref[:, cols] = out
        pooled = dot(onehot, out).astype(BF16)
        for i in range(copies):
            pooled_ref[i, :, cols] = pooled


def score(emb, cands, own, pos):
    scores = dot(cands, emb, NT, HIGHEST) / 0.05
    cidx = lax.broadcasted_iota(jnp.int32, scores.shape, 0)
    didx = lax.broadcasted_iota(jnp.int32, scores.shape, 1)
    total = jnp.sum(jnp.where(cidx != own + didx, jnp.exp(scores), 0.0), axis=0, keepdims=True)
    picked = jnp.sum(jnp.where(cidx == pos, scores, 0.0), axis=0, keepdims=True)
    return jnp.log(total) - picked


def loss_kernel(parts_ref, pos_ref, loss_ref):
    emb = unit(jnp.sum(parts_ref[...].astype(F32), axis=0))
    loss_ref[...] = score(emb, emb, 0, pos_ref[...])


VMEM = pl.BlockSpec(memory_space=pltpu.VMEM)
SMEM = pl.BlockSpec(memory_space=pltpu.SMEM)
HBM = pl.BlockSpec(memory_space=pltpu.HBM)


def call(body, outs, name, specs, flops=0, scratch=(), aliases={}):
    return pl.pallas_call(
        body,
        out_shape=[jax.ShapeDtypeStruct(s, d) for s, d in outs],
        in_specs=specs,
        out_specs=[VMEM] * len(outs),
        scratch_shapes=scratch,
        input_output_aliases=aliases,
        compiler_params=pltpu.CompilerParams(vmem_limit_bytes=40 << 20),
        cost_estimate=pl.CostEstimate(flops=flops, bytes_accessed=4 << 20, transcendentals=0),
        name=name,
    )


def on_device(rows_in, queries, keys, strengths, gates, doc_ids, positives, norm_gain):
    length, width = rows_in.shape[2], rows_in.shape[3]
    heads, ndoc = strengths.shape[2], positives.shape[2]
    subs = length // SUB
    half = heads // 2
    size, pipes, replicas = (lax.axis_size(x) for x in ("ctx", "pipe", "dp"))
    chips = size // 2
    reach = chips // 4
    v, q, k = rows_in[0, 0], queries[0, 0], keys[0, 0]
    beta, gate, ids = strengths[0, 0], gates[0, 0], doc_ids[0]
    core = (lax.axis_index("ctx") % 2).astype(jnp.int32).reshape(1)

    def swapped(x):
        return lax.ppermute(x, "ctx", [(i, i ^ 1) for i in range(size)])

    def from_behind(x, d):
        return lax.ppermute(x, "ctx", [(i, i + 2 * d) for i in range(size - 2 * d)])

    big = (heads * SUB + META, SUB)
    send, keep, wv, yy, p0, u0, k, v, gate, ids = call(
        functools.partial(chunk_kernel, heads, subs),
        [(big, BF16), (big, BF16), ((length, width), F32), ((length, width), BF16)]
        + [((heads * SUB, SUB), BF16)] * 2 + [((length, width), BF16)] * 2
        + [((heads, length), F32), ((1, length), jnp.int32)],
        "chunks", [SMEM] + [HBM] * 5, 1 << 31,
        [pltpu.VMEM((heads, length), F32), pltpu.SemaphoreType.DMA((3 + 2 * subs,))],
    )(core, *(pltpu.with_memory_space_constraint(x, pltpu.HBM) for x in (k, v, beta, gate, ids)))
    got = swapped(send)
    full, tail = call(
        functools.partial(pair_kernel, heads),
        [(big, BF16), ((half * SUB + META, SUB), BF16)],
        "pair", [SMEM, VMEM, VMEM], 1 << 25,
    )(core, keep, got)
    arrived = [from_behind(full, d) for d in range(1, reach)] + [from_behind(tail, reach)]
    local, reached, gain, pos = call(
        functools.partial(query_kernel, heads, subs),
        [((length, width), F32), ((length, width), BF16), (norm_gain.shape, F32), ((1, ndoc), jnp.int32)],
        "queries", [VMEM] * 10, 1 << 31,
    )(q, k, gate, ids, wv, yy, p0, u0, norm_gain, positives[0])
    arrived, local, reached, gain, pos = lax.optimization_barrier((arrived, local, reached, gain, pos))
    give, mine = call(
        functools.partial(enter_kernel, heads, reach),
        [((half * SUB, SUB), BF16)] * 2,
        "enter", [SMEM] + [VMEM] * (2 + reach), 1 << 25,
    )(core, keep, got, *arrived)
    theirs = swapped(give)
    outs = [((length, width), BF16), ((size, ndoc, width), BF16)]
    rest = (local, reached, v, gain, ids)
    begun = call(
        functools.partial(rows_kernel, heads, ndoc, size, True), outs, "rows_own", [SMEM] + [VMEM] * 6, 1 << 31
    )(core, mine, *rest)
    rows_out, pooled = call(
        functools.partial(rows_kernel, heads, ndoc, size, False), outs, "rows_other",
        [SMEM] + [VMEM] * 8, 1 << 26, aliases={7: 0, 8: 1},
    )(core, theirs, *rest, *begun)
    passed = lax.ppermute(rows_out, "pipe", [(i, (i + 1) % pipes) for i in range(pipes)])
    parts = lax.all_to_all(pooled, "ctx", 0, 0)
    if replicas == 1:
        (loss,) = call(loss_kernel, [((1, ndoc), F32)], "loss", [VMEM, VMEM])(parts, pos)
    else:
        mine = unit(jnp.sum(parts.astype(F32), axis=0))
        cands = lax.all_gather(mine.astype(BF16), "dp", axis=0, tiled=True).astype(F32)
        loss = score(mine, cands, lax.axis_index("dp") * ndoc, pos)
    return (passed.reshape(1, 1, length, width), loss.reshape(1, 1, ndoc))


def solution(mesh):
    rows = P(("groups", "pipe"), "dp", "ctx", None)
    tokens = P(("groups", "pipe"), "dp", None, "ctx")
    docs = P(("groups", "pipe"), "dp", None)
    in_specs = (
        rows, rows, rows, tokens, tokens, P(("groups", "pipe"), "dp", "ctx"), docs, P("pipe", None)
    )
    return jax.shard_map(
        on_device, mesh=mesh, in_specs=in_specs, out_specs=(rows, docs), check_vma=False
    )
```

```python
import functools

import jax
import jax.numpy as jnp
from jax import lax
from jax.experimental import pallas as pl
from jax.experimental.pallas import tpu as pltpu
from jax.sharding import PartitionSpec as P

F32, BF16 = jnp.float32, jnp.bfloat16
HIGHEST = lax.Precision.HIGHEST
NEG = -1e30
SUB = 128
META = 16

NN = (((1,), (0,)), ((), ()))
NT = (((1,), (1,)), ((), ()))
TN = (((0,), (0,)), ((), ()))


def dot(a, b, dims=NN, precision=None):
    return lax.dot_general(a, b, dims, precision=precision, preferred_element_type=F32)


def dot1(a, b, dims=NN):
    return dot(a.astype(BF16), b.astype(BF16), dims)


def split(x):
    high = x.astype(BF16)
    return high, (x - high.astype(F32)).astype(BF16)


def dot3(a, b, dims=NN):
    (ah, al), (bh, bl) = split(a), split(b)
    return dot(ah, bh, dims) + (dot(al, bh, dims) + dot(ah, bl, dims))


def unit(x):
    return x * lax.rsqrt(jnp.sum(x * x, axis=-1, keepdims=True) + 1e-06)


def iotas():
    shape = (SUB, SUB)
    return lax.broadcasted_iota(jnp.int32, shape, 0), lax.broadcasted_iota(jnp.int32, shape, 1)


def per_token(rows, heads, subs):
    return jnp.concatenate([rows[:, j * SUB : (j + 1) * SUB] for j in range(subs)], axis=0)


class Decay:
    def __init__(self, gates, ids, heads, subs):
        r, c = iotas()
        upto = (c <= r).astype(F32)
        logs = per_token(jnp.log(gates), heads, subs)
        self.row = dot(logs, upto, NT, HIGHEST)
        self.col = dot(upto, logs, NT, HIGHEST)
        ids = ids.astype(F32)
        self.eye = (r == c).astype(F32)
        self.id_row = [ids[:, j * SUB : (j + 1) * SUB] for j in range(subs)]
        stacked = jnp.concatenate([jnp.broadcast_to(x, (8, SUB)) for x in self.id_row], axis=0)
        turned = dot1(self.eye, stacked, NT)
        self.id_col = [turned[:, 8 * j : 8 * j + 1] for j in range(subs)]
        self.heads, self.r, self.c = heads, r, c
        lead, tail = [], []
        for j in range(subs):
            row, last = self.row[j * heads : (j + 1) * heads], self.id_row[j][:, SUB - 1 :]
            entry = self.id_row[0][:, :1] if j == 0 else self.id_row[j - 1][:, SUB - 1 :]
            lead.append(jnp.where(self.id_row[j] == entry, jnp.exp(row), 0.0))
            tail.append(jnp.exp(jnp.where(self.id_row[j] == last, row[:, SUB - 1 :] - row, NEG)))
        self.lead = jnp.concatenate(lead, axis=0)
        self.tail = jnp.concatenate(tail, axis=0)
        self.same = [(x == y) & (r >= c) for x, y in zip(self.id_col, self.id_row)]

    def inner(self, h, j, keep):
        i = j * self.heads + h
        return jnp.exp(jnp.where(keep[j], self.col[:, i : i + 1] - self.row[i : i + 1, :], NEG))


def block(ref, h, j):
    return ref[j * SUB : (j + 1) * SUB, h * SUB : (h + 1) * SUB]


def chunk_kernel(
    heads, subs, core_ref, k_hbm, v_hbm, beta_hbm, gates_hbm, ids_hbm,
    send_ref, keep_ref, wv_ref, yy_ref, p0_ref, u0_ref, k_ref, v_ref,
    beta_ref, gates_ref, ids_ref, sems,
):
    small = [(gates_hbm, gates_ref), (ids_hbm, ids_ref), (beta_hbm, beta_ref)]
    parts = [pl.ds(j * SUB, SUB) for j in range(subs)]
    large = [(x.at[p, :], y.at[p, :]) for x, y in ((k_hbm, k_ref), (v_hbm, v_ref)) for p in parts]
    copies = [pltpu.make_async_copy(x, y, sems.at[i]) for i, (x, y) in enumerate(small + large)]
    for copy in copies:
        copy.start()
    for copy in copies[:3]:
        copy.wait()
    decay = Decay(gates_ref[...], ids_ref[...], heads, subs)
    r, c, eye = decay.r, decay.c, decay.eye
    beta = per_token(beta_ref[...], heads, subs)
    tails = decay.tail * beta
    strict = [x & (r > c) for x in decay.same]
    chains = [(h, j) for j in range(subs) for h in range(heads)]
    kn, kt, low, inv = {}, {}, {}, {}
    for h, j in chains:
        if h == 0:
            copies[3 + j].wait()
        unit_keys = unit(block(k_ref, h, j).astype(F32))
        kn[h, j] = unit_keys.astype(BF16)
        kt[h, j] = unit_keys.T
    near = ((r // 2) == (c // 2)) & (r > c)
    for h, j in chains:
        i = j * heads + h
        gram = dot(kn[h, j], kt[h, j].astype(BF16))
        full = decay.inner(h, j, strict) * gram * beta[i : i + 1, :]
        inv[h, j] = eye - jnp.where(near, full, 0.0)
        low[h, j] = full.astype(BF16)
    size = 2
    while size < SUB:
        pick = (((r // size) % 2 == 1) & ((c // size) == (r // size) - 1)).astype(BF16)
        odd = range(size, SUB, 2 * size)
        half, rows = {}, {}
        for key in chains:
            rows[key] = inv[key]
            if size >= 8:
                rows[key] = jnp.concatenate([inv[key][o : o + size] for o in odd], axis=0)
            half[key] = dot1(rows[key], low[key] * pick)
        for key in chains:
            new = rows[key] - dot1(half[key], inv[key])
            if size >= 8:
                parts = []
                for n, o in enumerate(odd):
                    parts += [inv[key][o - size : o], new[n * size : (n + 1) * size]]
                new = jnp.concatenate(parts, axis=0)
            inv[key] = new
        size *= 2
    for copy in copies[3 + subs :]:
        copy.wait()
    wv, yy, pp, uu = {}, {}, {}, {}
    for h, j in chains:
        i = j * heads + h
        xh, xl = split(inv[h, j])
        values = block(v_ref, h, j)
        wv[h, j] = dot(xh, values) + dot(xl, values)
        yy[h, j] = dot((inv[h, j] * decay.lead[i : i + 1, :]).astype(BF16), kn[h, j]).astype(BF16)
        wv_ref[j * SUB : (j + 1) * SUB, h * SUB : (h + 1) * SUB] = wv[h, j]
        yy_ref[j * SUB : (j + 1) * SUB, h * SUB : (h + 1) * SUB] = yy[h, j]
    for h, j in chains:
        i = j * heads + h
        dh, dl = split(kt[h, j] * tails[i : i + 1, :])
        wh, wl = split(wv[h, j])
        got = dot(dh, jnp.concatenate([wh, yy[h, j]], axis=1))
        pp[h, j] = decay.lead[i : i + 1, SUB - 1 :] * eye - got[:, SUB:]
        uu[h, j] = got[:, :SUB] + (dot(dl, wh) + dot(dh, wl))
    for h in range(heads):
        p0, u0 = pp[h, 0].astype(BF16), uu[h, 0].astype(BF16)
        p0_ref[h * SUB : (h + 1) * SUB, :] = p0
        u0_ref[h * SUB : (h + 1) * SUB, :] = u0
        for j in range(1, subs):
            got = dot1(pp[h, j], jnp.concatenate([u0, p0], axis=1))
            uu[h, 0] = uu[h, j] + got[:, :SUB]
            pp[h, 0] = got[:, SUB:]
            u0, p0 = uu[h, 0].astype(BF16), pp[h, 0].astype(BF16)
    half_heads = heads // 2
    first = core_ref[0] == 0
    for h in range(half_heads):
        for base, part in ((0, pp), (half_heads, uu)):
            lo, hi = part[h, 0].astype(BF16), part[half_heads + h, 0].astype(BF16)
            at = slice((base + h) * SUB, (base + h + 1) * SUB)
            send_ref[at, :] = jnp.where(first, hi, lo)
            keep_ref[at, :] = jnp.where(first, lo, hi)
    start = decay.id_row[0][:, :1]
    end = decay.id_row[-1][:, SUB - 1 :]
    which = lax.broadcasted_iota(jnp.int32, (META, SUB), 0) < META // 2
    meta = jnp.where(which, end, start).astype(BF16)
    send_ref[heads * SUB :, :] = meta
    keep_ref[heads * SUB :, :] = meta


def query_kernel(
    heads, subs, q_ref, k_ref, beta_ref, gates_ref, ids_ref, wv_ref, yy_ref, p0_ref, u0_ref,
    gain_in, pos_in, local_ref, reach_ref, gain_ref, pos_ref,
):
    gain_ref[...] = gain_in[...]
    pos_ref[...] = pos_in[...]
    decay = Decay(gates_ref[...], ids_ref[...], heads, subs)
    beta = per_token(beta_ref[...], heads, subs)
    lead = dot(decay.eye, decay.lead, NT, HIGHEST)
    chains = [(h, j) for j in range(subs) for h in range(heads)]
    qn, attend, reach, local = {}, {}, {}, {}
    for h, j in chains:
        i = j * heads + h
        qn[h, j] = unit(block(q_ref, h, j).astype(F32))
        kn = unit(block(k_ref, h, j).astype(F32))
        attend[h, j] = decay.inner(h, j, decay.same) * dot3(qn[h, j], kn, NT) * beta[i : i + 1, :]
    for h, j in chains:
        i = j * heads + h
        ah, al = split(attend[h, j])
        wh, wl = split(block(wv_ref, h, j))
        reach[h, j] = lead[:, i : i + 1] * qn[h, j] - dot(ah, block(yy_ref, h, j))
        local[h, j] = dot(ah, wh) + (dot(al, wh) + dot(ah, wl))
    for h, j in chains:
        if j > 0:
            rb = reach[h, j].astype(BF16)
            at = slice(h * SUB, (h + 1) * SUB)
            local[h, j] = local[h, j] + dot(rb, u0_ref[at, :])
            reach[h, j] = dot(rb, p0_ref[at, :])
        local_ref[j * SUB : (j + 1) * SUB, h * SUB : (h + 1) * SUB] = local[h, j]
        reach_ref[j * SUB : (j + 1) * SUB, h * SUB : (h + 1) * SUB] = reach[h, j].astype(BF16)


def ends(ref, rows):
    meta = ref[rows : rows + META, :].astype(F32)
    return meta[META // 2 : META // 2 + 1, :], meta[:1, :]


def pair_kernel(heads, core_ref, keep_ref, got_ref, full_ref, tail_ref):
    half = heads // 2
    first = core_ref[0] == 0
    own, other = ends(keep_ref, heads * SUB), ends(got_ref, heads * SUB)
    early = [jnp.where(first, a, b) for a, b in zip(own, other)]
    late = [jnp.where(first, b, a) for a, b in zip(own, other)]
    joined = (early[1] == late[0]).astype(F32)
    for h in range(half):
        at, up = slice(h * SUB, (h + 1) * SUB), slice((half + h) * SUB, (half + h + 1) * SUB)
        p1 = jnp.where(first, keep_ref[at, :], got_ref[at, :])
        p2 = jnp.where(first, got_ref[at, :], keep_ref[at, :])
        u1 = jnp.where(first, keep_ref[up, :], got_ref[up, :])
        u2 = jnp.where(first, got_ref[up, :], keep_ref[up, :])
        full_ref[at, :] = (joined * dot(p2, p1)).astype(BF16)
        state = (u2.astype(F32) + joined * dot(p2, u1)).astype(BF16)
        full_ref[up, :] = state
        tail_ref[at, :] = state
    which = lax.broadcasted_iota(jnp.int32, (META, SUB), 0) < META // 2
    meta = jnp.where(which, late[1], early[0]).astype(BF16)
    full_ref[heads * SUB :, :] = meta
    tail_ref[half * SUB :, :] = meta


def enter_kernel(heads, reach, core_ref, keep_ref, got_ref, *refs):
    chips, (send_ref, mine_ref) = refs[:reach], refs[reach:]
    half = heads // 2
    first = core_ref[0] == 0
    own, other = ends(keep_ref, heads * SUB), ends(got_ref, heads * SUB)
    early = [jnp.where(first, a, b) for a, b in zip(own, other)]
    late = [jnp.where(first, b, a) for a, b in zip(own, other)]
    marks = [(early[0], None)]
    for d, ref in enumerate(chips):
        marks.append(ends(ref, (heads if d < reach - 1 else half) * SUB))
    links = [(marks[d][0] == marks[d + 1][1]).astype(F32) for d in range(reach)]
    joined = (early[1] == late[0]).astype(F32)
    for h in range(half):
        at, up = slice(h * SUB, (h + 1) * SUB), slice((half + h) * SUB, (half + h + 1) * SUB)
        state = chips[-1][at, :].astype(F32)
        for d in range(reach - 2, -1, -1):
            state = chips[d][up, :].astype(F32) + links[d + 1] * dot1(chips[d][at, :], state)
        state = (links[0] * state).astype(BF16)
        p1 = jnp.where(first, keep_ref[at, :], got_ref[at, :])
        u1 = jnp.where(first, keep_ref[up, :], got_ref[up, :])
        middle = (joined * (u1.astype(F32) + dot(p1, state))).astype(BF16)
        send_ref[at, :] = jnp.where(first, middle, state)
        mine_ref[at, :] = jnp.where(first, state, middle)


def rows_kernel(
    heads, ndoc, copies, own, core_ref, state_ref, local_ref, reach_ref, v_ref, gain_ref, ids_ref, *refs
):
    out_ref, pooled_ref = refs[-2:]
    half = heads // 2
    group = core_ref[0] if own else 1 - core_ref[0]
    docs = lax.broadcasted_iota(jnp.int32, (ndoc, v_ref.shape[0]), 0)
    onehot = (docs == ids_ref[...]).astype(F32).astype(BF16)
    gain = gain_ref[...]
    for h in range(half):
        cols = pl.ds(pl.multiple_of((group * half + h) * SUB, SUB), SUB)
        o = local_ref[:, cols] + dot(reach_ref[:, cols], state_ref[h * SUB : (h + 1) * SUB, :])
        scale = lax.rsqrt(jnp.sum(o * o, axis=-1, keepdims=True) * (1.0 / SUB) + 1e-06)
        out = (v_ref[:, cols].astype(F32) + o * scale * gain).astype(BF16)
        out_ref[:, cols] = out
        pooled = dot(onehot, out).astype(BF16)
        for i in range(copies):
            pooled_ref[i, :, cols] = pooled


def score(emb, cands, own, pos):
    scores = dot(cands, emb, NT, HIGHEST) / 0.05
    cidx = lax.broadcasted_iota(jnp.int32, scores.shape, 0)
    didx = lax.broadcasted_iota(jnp.int32, scores.shape, 1)
    total = jnp.sum(jnp.where(cidx != own + didx, jnp.exp(scores), 0.0), axis=0, keepdims=True)
    picked = jnp.sum(jnp.where(cidx == pos, scores, 0.0), axis=0, keepdims=True)
    return jnp.log(total) - picked


def loss_kernel(parts_ref, pos_ref, loss_ref):
    emb = unit(jnp.sum(parts_ref[...].astype(F32), axis=0))
    loss_ref[...] = score(emb, emb, 0, pos_ref[...])


VMEM = pl.BlockSpec(memory_space=pltpu.VMEM)
SMEM = pl.BlockSpec(memory_space=pltpu.SMEM)
HBM = pl.BlockSpec(memory_space=pltpu.HBM)


def call(body, outs, name, specs, flops=0, scratch=(), aliases={}):
    return pl.pallas_call(
        body,
        out_shape=[jax.ShapeDtypeStruct(s, d) for s, d in outs],
        in_specs=specs,
        out_specs=[VMEM] * len(outs),
        scratch_shapes=scratch,
        input_output_aliases=aliases,
        compiler_params=pltpu.CompilerParams(vmem_limit_bytes=40 << 20),
        cost_estimate=pl.CostEstimate(flops=flops, bytes_accessed=4 << 20, transcendentals=0),
        name=name,
    )


def on_device(rows_in, queries, keys, strengths, gates, doc_ids, positives, norm_gain):
    length, width = rows_in.shape[2], rows_in.shape[3]
    heads, ndoc = strengths.shape[2], positives.shape[2]
    subs = length // SUB
    half = heads // 2
    size, pipes, replicas = (lax.axis_size(x) for x in ("ctx", "pipe", "dp"))
    chips = size // 2
    reach = chips // 4
    v, q, k = rows_in[0, 0], queries[0, 0], keys[0, 0]
    beta, gate, ids = strengths[0, 0], gates[0, 0], doc_ids[0]
    core = (lax.axis_index("ctx") % 2).astype(jnp.int32).reshape(1)

    def swapped(x):
        return lax.ppermute(x, "ctx", [(i, i ^ 1) for i in range(size)])

    def from_behind(x, d):
        return lax.ppermute(x, "ctx", [(i, i + 2 * d) for i in range(size - 2 * d)])

    big = (heads * SUB + META, SUB)
    send, keep, wv, yy, p0, u0, k, v, beta, gate, ids = call(
        functools.partial(chunk_kernel, heads, subs),
        [(big, BF16), (big, BF16), ((length, width), F32), ((length, width), BF16)]
        + [((heads * SUB, SUB), BF16)] * 2 + [((length, width), BF16)] * 2
        + [((heads, length), F32)] * 2 + [((1, length), jnp.int32)],
        "chunks", [SMEM] + [HBM] * 5, 1 << 31,
        [pltpu.SemaphoreType.DMA((3 + 2 * subs,))],
    )(core, *(pltpu.with_memory_space_constraint(x, pltpu.HBM) for x in (k, v, beta, gate, ids)))
    got = swapped(send)
    full, tail = call(
        functools.partial(pair_kernel, heads),
        [(big, BF16), ((half * SUB + META, SUB), BF16)],
        "pair", [SMEM, VMEM, VMEM], 1 << 25,
    )(core, keep, got)
    arrived = [from_behind(full, d) for d in range(1, reach)] + [from_behind(tail, reach)]
    local, reached, gain, pos = call(
        functools.partial(query_kernel, heads, subs),
        [((length, width), F32), ((length, width), BF16), (norm_gain.shape, F32), ((1, ndoc), jnp.int32)],
        "queries", [VMEM] * 11, 1 << 31,
    )(q, k, beta, gate, ids, wv, yy, p0, u0, norm_gain, positives[0])
    arrived, local, reached, gain, pos = lax.optimization_barrier((arrived, local, reached, gain, pos))
    give, mine = call(
        functools.partial(enter_kernel, heads, reach),
        [((half * SUB, SUB), BF16)] * 2,
        "enter", [SMEM] + [VMEM] * (2 + reach), 1 << 25,
    )(core, keep, got, *arrived)
    theirs = swapped(give)
    outs = [((length, width), BF16), ((size, ndoc, width), BF16)]
    rest = (local, reached, v, gain, ids)
    begun = call(
        functools.partial(rows_kernel, heads, ndoc, size, True), outs, "rows_own", [SMEM] + [VMEM] * 6, 1 << 31
    )(core, mine, *rest)
    rows_out, pooled = call(
        functools.partial(rows_kernel, heads, ndoc, size, False), outs, "rows_other",
        [SMEM] + [VMEM] * 8, 1 << 26, aliases={7: 0, 8: 1},
    )(core, theirs, *rest, *begun)
    passed = lax.ppermute(rows_out, "pipe", [(i, (i + 1) % pipes) for i in range(pipes)])
    parts = lax.all_to_all(pooled, "ctx", 0, 0)
    if replicas == 1:
        (loss,) = call(loss_kernel, [((1, ndoc), F32)], "loss", [VMEM, VMEM])(parts, pos)
    else:
        mine = unit(jnp.sum(parts.astype(F32), axis=0))
        cands = lax.all_gather(mine.astype(BF16), "dp", axis=0, tiled=True).astype(F32)
        loss = score(mine, cands, lax.axis_index("dp") * ndoc, pos)
    return (passed.reshape(1, 1, length, width), loss.reshape(1, 1, ndoc))


def solution(mesh):
    rows = P(("groups", "pipe"), "dp", "ctx", None)
    tokens = P(("groups", "pipe"), "dp", None, "ctx")
    docs = P(("groups", "pipe"), "dp", None)
    in_specs = (
        rows, rows, rows, tokens, tokens, P(("groups", "pipe"), "dp", "ctx"), docs, P("pipe", None)
    )
    return jax.shard_map(
        on_device, mesh=mesh, in_specs=in_specs, out_specs=(rows, docs), check_vma=False
    )
```

```python
import functools

import jax
import jax.numpy as jnp
from jax import lax
from jax.experimental import pallas as pl
from jax.experimental.pallas import tpu as pltpu
from jax.sharding import PartitionSpec as P

F32, BF16 = jnp.float32, jnp.bfloat16
HIGHEST = lax.Precision.HIGHEST
NEG = -1e30
SUB = 128
META = 16

NN = (((1,), (0,)), ((), ()))
NT = (((1,), (1,)), ((), ()))
TN = (((0,), (0,)), ((), ()))


def dot(a, b, dims=NN, precision=None):
    return lax.dot_general(a, b, dims, precision=precision, preferred_element_type=F32)


def dot1(a, b, dims=NN):
    return dot(a.astype(BF16), b.astype(BF16), dims)


def split(x):
    high = x.astype(BF16)
    return high, (x - high.astype(F32)).astype(BF16)


def dot3(a, b, dims=NN):
    (ah, al), (bh, bl) = split(a), split(b)
    return dot(ah, bh, dims) + (dot(al, bh, dims) + dot(ah, bl, dims))


def unit(x):
    return x * lax.rsqrt(jnp.sum(x * x, axis=-1, keepdims=True) + 1e-06)


def iotas():
    shape = (SUB, SUB)
    return lax.broadcasted_iota(jnp.int32, shape, 0), lax.broadcasted_iota(jnp.int32, shape, 1)


def per_token(rows, heads, subs):
    return jnp.concatenate([rows[:, j * SUB : (j + 1) * SUB] for j in range(subs)], axis=0)


class Decay:
    def __init__(self, gates, ids, heads, subs):
        r, c = iotas()
        upto = (c <= r).astype(F32)
        logs = per_token(jnp.log(gates), heads, subs)
        self.row = dot(logs, upto, NT, HIGHEST)
        self.col = dot(upto, logs, NT, HIGHEST)
        ids = ids.astype(F32)
        self.eye = (r == c).astype(F32)
        self.id_row = [ids[:, j * SUB : (j + 1) * SUB] for j in range(subs)]
        stacked = jnp.concatenate([jnp.broadcast_to(x, (8, SUB)) for x in self.id_row], axis=0)
        turned = dot1(self.eye, stacked, NT)
        self.id_col = [turned[:, 8 * j : 8 * j + 1] for j in range(subs)]
        self.heads, self.r, self.c = heads, r, c
        lead, tail = [], []
        for j in range(subs):
            row, last = self.row[j * heads : (j + 1) * heads], self.id_row[j][:, SUB - 1 :]
            entry = self.id_row[0][:, :1] if j == 0 else self.id_row[j - 1][:, SUB - 1 :]
            lead.append(jnp.where(self.id_row[j] == entry, jnp.exp(row), 0.0))
            tail.append(jnp.exp(jnp.where(self.id_row[j] == last, row[:, SUB - 1 :] - row, NEG)))
        self.lead = jnp.concatenate(lead, axis=0)
        self.tail = jnp.concatenate(tail, axis=0)
        self.same = [(x == y) & (r >= c) for x, y in zip(self.id_col, self.id_row)]

    def inner(self, h, j, keep):
        i = j * self.heads + h
        return jnp.exp(jnp.where(keep[j], self.col[:, i : i + 1] - self.row[i : i + 1, :], NEG))


def block(ref, h, j):
    return ref[j * SUB : (j + 1) * SUB, h * SUB : (h + 1) * SUB]


def chunk_kernel(
    heads, subs, core_ref, k_hbm, v_hbm, beta_hbm, gates_hbm, ids_hbm,
    send_ref, keep_ref, wv_ref, yy_ref, p0_ref, u0_ref, k_ref, v_ref,
    beta_ref, gates_ref, ids_ref, sems,
):
    small = [(gates_hbm, gates_ref), (ids_hbm, ids_ref), (beta_hbm, beta_ref)]
    parts = [pl.ds(j * SUB, SUB) for j in range(subs)]
    large = [(x.at[p, :], y.at[p, :]) for x, y in ((k_hbm, k_ref), (v_hbm, v_ref)) for p in parts]
    copies = [pltpu.make_async_copy(x, y, sems.at[i]) for i, (x, y) in enumerate(small + large)]
    for copy in copies:
        copy.start()
    for copy in copies[:3]:
        copy.wait()
    decay = Decay(gates_ref[...], ids_ref[...], heads, subs)
    r, c, eye = decay.r, decay.c, decay.eye
    beta = per_token(beta_ref[...], heads, subs)
    tails = decay.tail * beta
    strict = [x & (r > c) for x in decay.same]
    chains = [(h, j) for j in range(subs) for h in range(heads)]
    kn, kt, low, inv = {}, {}, {}, {}
    for h, j in chains:
        if h == 0:
            copies[3 + j].wait()
        unit_keys = unit(block(k_ref, h, j).astype(F32))
        kn[h, j] = unit_keys.astype(BF16)
        kt[h, j] = unit_keys.T
    near = ((r // 2) == (c // 2)) & (r > c)
    for h, j in chains:
        i = j * heads + h
        gram = dot(kn[h, j], kt[h, j].astype(BF16))
        full = decay.inner(h, j, strict) * gram * beta[i : i + 1, :]
        inv[h, j] = eye - jnp.where(near, full, 0.0)
        low[h, j] = full.astype(BF16)
    size = 2
    while size < SUB:
        pick = (((r // size) % 2 == 1) & ((c // size) == (r // size) - 1)).astype(BF16)
        odd = range(size, SUB, 2 * size)
        half, rows = {}, {}
        for key in chains:
            rows[key] = inv[key]
            if size >= 8:
                rows[key] = jnp.concatenate([inv[key][o : o + size] for o in odd], axis=0)
            half[key] = dot1(rows[key], low[key] * pick)
        for key in chains:
            new = rows[key] - dot1(half[key], inv[key])
            if size >= 8:
                parts = []
                for n, o in enumerate(odd):
                    parts += [inv[key][o - size : o], new[n * size : (n + 1) * size]]
                new = jnp.concatenate(parts, axis=0)
            inv[key] = new
        size *= 2
    for copy in copies[3 + subs :]:
        copy.wait()
    wv, yy, pp, uu = {}, {}, {}, {}
    for h, j in chains:
        i = j * heads + h
        xh, xl = split(inv[h, j])
        values = block(v_ref, h, j)
        wv[h, j] = dot(xh, values) + dot(xl, values)
        yy[h, j] = dot((inv[h, j] * decay.lead[i : i + 1, :]).astype(BF16), kn[h, j]).astype(BF16)
        wv_ref[j * SUB : (j + 1) * SUB, h * SUB : (h + 1) * SUB] = wv[h, j]
        yy_ref[j * SUB : (j + 1) * SUB, h * SUB : (h + 1) * SUB] = yy[h, j]
    for h, j in chains:
        i = j * heads + h
        dh, dl = split(kt[h, j] * tails[i : i + 1, :])
        wh, wl = split(wv[h, j])
        got = dot(dh, jnp.concatenate([wh, yy[h, j]], axis=1))
        pp[h, j] = decay.lead[i : i + 1, SUB - 1 :] * eye - got[:, SUB:]
        uu[h, j] = got[:, :SUB] + (dot(dl, wh) + dot(dh, wl))
    for h in range(heads):
        p0, u0 = pp[h, 0].astype(BF16), uu[h, 0].astype(BF16)
        p0_ref[h * SUB : (h + 1) * SUB, :] = p0
        u0_ref[h * SUB : (h + 1) * SUB, :] = u0
        for j in range(1, subs):
            got = dot1(pp[h, j], jnp.concatenate([u0, p0], axis=1))
            uu[h, 0] = uu[h, j] + got[:, :SUB]
            pp[h, 0] = got[:, SUB:]
            u0, p0 = uu[h, 0].astype(BF16), pp[h, 0].astype(BF16)
    half_heads = heads // 2
    first = core_ref[0] == 0
    for h in range(half_heads):
        for base, part in ((0, pp), (half_heads, uu)):
            lo, hi = part[h, 0].astype(BF16), part[half_heads + h, 0].astype(BF16)
            at = slice((base + h) * SUB, (base + h + 1) * SUB)
            send_ref[at, :] = jnp.where(first, hi, lo)
            keep_ref[at, :] = jnp.where(first, lo, hi)
    start = decay.id_row[0][:, :1]
    end = decay.id_row[-1][:, SUB - 1 :]
    which = lax.broadcasted_iota(jnp.int32, (META, SUB), 0) < META // 2
    meta = jnp.where(which, end, start).astype(BF16)
    send_ref[heads * SUB :, :] = meta
    keep_ref[heads * SUB :, :] = meta


def query_kernel(
    heads, subs, q_ref, k_ref, beta_ref, gates_ref, ids_ref, wv_ref, yy_ref, p0_ref, u0_ref,
    gain_in, pos_in, local_ref, reach_ref, gain_ref, pos_ref,
):
    gain_ref[...] = gain_in[...]
    pos_ref[...] = pos_in[...]
    decay = Decay(gates_ref[...], ids_ref[...], heads, subs)
    beta = per_token(beta_ref[...], heads, subs)
    lead = dot(decay.eye, decay.lead, NT, HIGHEST)
    chains = [(h, j) for j in range(subs) for h in range(heads)]
    qn, attend, reach, local = {}, {}, {}, {}
    for h, j in chains:
        i = j * heads + h
        qn[h, j] = unit(block(q_ref, h, j).astype(F32))
        kn = unit(block(k_ref, h, j).astype(F32))
        attend[h, j] = decay.inner(h, j, decay.same) * dot3(qn[h, j], kn, NT) * beta[i : i + 1, :]
    for h, j in chains:
        i = j * heads + h
        ah, al = split(attend[h, j])
        wh, wl = split(block(wv_ref, h, j))
        reach[h, j] = lead[:, i : i + 1] * qn[h, j] - dot(ah, block(yy_ref, h, j))
        local[h, j] = dot(ah, wh) + (dot(al, wh) + dot(ah, wl))
    for h, j in chains:
        if j > 0:
            rb = reach[h, j].astype(BF16)
            at = slice(h * SUB, (h + 1) * SUB)
            local[h, j] = local[h, j] + dot(rb, u0_ref[at, :])
            reach[h, j] = dot(rb, p0_ref[at, :])
        local_ref[j * SUB : (j + 1) * SUB, h * SUB : (h + 1) * SUB] = local[h, j]
        reach_ref[j * SUB : (j + 1) * SUB, h * SUB : (h + 1) * SUB] = reach[h, j].astype(BF16)


def ends(ref, rows):
    meta = ref[rows : rows + META, :].astype(F32)
    return meta[META // 2 : META // 2 + 1, :], meta[:1, :]


def pair_kernel(heads, core_ref, keep_ref, got_ref, full_ref, tail_ref):
    half = heads // 2
    first = core_ref[0] == 0
    own, other = ends(keep_ref, heads * SUB), ends(got_ref, heads * SUB)
    early = [jnp.where(first, a, b) for a, b in zip(own, other)]
    late = [jnp.where(first, b, a) for a, b in zip(own, other)]
    joined = (early[1] == late[0]).astype(F32)
    for h in range(half):
        at, up = slice(h * SUB, (h + 1) * SUB), slice((half + h) * SUB, (half + h + 1) * SUB)
        p1 = jnp.where(first, keep_ref[at, :], got_ref[at, :])
        p2 = jnp.where(first, got_ref[at, :], keep_ref[at, :])
        u1 = jnp.where(first, keep_ref[up, :], got_ref[up, :])
        u2 = jnp.where(first, got_ref[up, :], keep_ref[up, :])
        full_ref[at, :] = (joined * dot(p2, p1)).astype(BF16)
        state = (u2.astype(F32) + joined * dot(p2, u1)).astype(BF16)
        full_ref[up, :] = state
        tail_ref[at, :] = state
    which = lax.broadcasted_iota(jnp.int32, (META, SUB), 0) < META // 2
    meta = jnp.where(which, late[1], early[0]).astype(BF16)
    full_ref[heads * SUB :, :] = meta
    tail_ref[half * SUB :, :] = meta


def enter_kernel(heads, reach, core_ref, keep_ref, got_ref, *refs):
    chips, (send_ref, mine_ref) = refs[:reach], refs[reach:]
    half = heads // 2
    first = core_ref[0] == 0
    own, other = ends(keep_ref, heads * SUB), ends(got_ref, heads * SUB)
    early = [jnp.where(first, a, b) for a, b in zip(own, other)]
    late = [jnp.where(first, b, a) for a, b in zip(own, other)]
    marks = [(early[0], None)]
    for d, ref in enumerate(chips):
        marks.append(ends(ref, (heads if d < reach - 1 else half) * SUB))
    links = [(marks[d][0] == marks[d + 1][1]).astype(F32) for d in range(reach)]
    joined = (early[1] == late[0]).astype(F32)
    for h in range(half):
        at, up = slice(h * SUB, (h + 1) * SUB), slice((half + h) * SUB, (half + h + 1) * SUB)
        state = chips[-1][at, :].astype(F32)
        for d in range(reach - 2, -1, -1):
            state = chips[d][up, :].astype(F32) + links[d + 1] * dot1(chips[d][at, :], state)
        state = (links[0] * state).astype(BF16)
        p1 = jnp.where(first, keep_ref[at, :], got_ref[at, :])
        u1 = jnp.where(first, keep_ref[up, :], got_ref[up, :])
        middle = (joined * (u1.astype(F32) + dot(p1, state))).astype(BF16)
        send_ref[at, :] = jnp.where(first, middle, state)
        mine_ref[at, :] = jnp.where(first, state, middle)


def rows_kernel(
    heads, ndoc, own, core_ref, state_ref, local_ref, reach_ref, v_ref, gain_ref, ids_ref, *refs
):
    out_ref, pooled_ref = refs[-2:]
    half = heads // 2
    group = core_ref[0] if own else 1 - core_ref[0]
    docs = lax.broadcasted_iota(jnp.int32, (ndoc, v_ref.shape[0]), 0)
    onehot = (docs == ids_ref[...]).astype(F32).astype(BF16)
    gain = gain_ref[...]
    mean = jnp.full((SUB, SUB), 1.0 / SUB, BF16)
    for h in range(half):
        cols = pl.ds(pl.multiple_of((group * half + h) * SUB, SUB), SUB)
        o = local_ref[:, cols] + dot(reach_ref[:, cols], state_ref[h * SUB : (h + 1) * SUB, :])
        scale = lax.rsqrt(dot1(o * o, mean) + 1e-06)
        out = (v_ref[:, cols].astype(F32) + o * scale * gain).astype(BF16)
        out_ref[:, cols] = out
        pooled_ref[:, cols] = dot(onehot, out).astype(BF16)


def losses(scores, own, pos):
    cidx = lax.broadcasted_iota(jnp.int32, scores.shape, 0)
    didx = lax.broadcasted_iota(jnp.int32, scores.shape, 1)
    total = jnp.sum(jnp.where(cidx != own + didx, jnp.exp(scores), 0.0), axis=0, keepdims=True)
    picked = jnp.sum(jnp.where(cidx == pos, scores, 0.0), axis=0, keepdims=True)
    return jnp.log(total) - picked


def add_kernel(a_ref, b_ref, out_ref):
    total = (a_ref[...].astype(F32) + b_ref[...].astype(F32)).astype(BF16)
    for i in range(out_ref.shape[0]):
        out_ref[i] = total


def store_rows(rows_ref, out_ref, sems):
    pieces = sems.shape[0]
    step = rows_ref.shape[0] // pieces
    at = [pl.ds(i * step, step) for i in range(pieces)]
    return [pltpu.make_async_copy(rows_ref.at[x, :], out_ref.at[x, :], sems.at[i]) for i, x in enumerate(at)]


def final_kernel(parts_ref, pos_ref, rows_ref, loss_out, out_ref, loss_ref, sems, loss_sem):
    copies = store_rows(rows_ref, out_ref, sems)
    for copy in copies:
        copy.start()
    sums = jnp.sum(parts_ref[...].astype(F32), axis=0)
    gram = dot(sums, sums, NT, HIGHEST)
    cidx = lax.broadcasted_iota(jnp.int32, gram.shape, 0)
    didx = lax.broadcasted_iota(jnp.int32, gram.shape, 1)
    squares = jnp.where(cidx == didx, gram, 0.0)
    across = lax.rsqrt(jnp.sum(squares, axis=0, keepdims=True) + 1e-06)
    down = lax.rsqrt(jnp.sum(squares, axis=1, keepdims=True) + 1e-06)
    loss_ref[...] = losses(gram * across * down / 0.05, 0, pos_ref[...])
    copies.append(pltpu.make_async_copy(loss_ref, loss_out, loss_sem))
    copies[-1].start()
    for copy in copies:
        copy.wait()


VMEM = pl.BlockSpec(memory_space=pltpu.VMEM)
SMEM = pl.BlockSpec(memory_space=pltpu.SMEM)
HBM = pl.BlockSpec(memory_space=pltpu.HBM)


def call(body, outs, name, specs, flops=0, scratch=(), aliases={}):
    return pl.pallas_call(
        body,
        out_shape=[jax.ShapeDtypeStruct(s, d) for s, d in outs],
        in_specs=specs,
        out_specs=[VMEM] * len(outs),
        scratch_shapes=scratch,
        input_output_aliases=aliases,
        compiler_params=pltpu.CompilerParams(vmem_limit_bytes=40 << 20),
        cost_estimate=pl.CostEstimate(flops=flops, bytes_accessed=4 << 20, transcendentals=0),
        name=name,
    )


def on_device(rows_in, queries, keys, strengths, gates, doc_ids, positives, norm_gain):
    length, width = rows_in.shape[2], rows_in.shape[3]
    heads, ndoc = strengths.shape[2], positives.shape[2]
    subs = length // SUB
    half = heads // 2
    size, pipes, replicas = (lax.axis_size(x) for x in ("ctx", "pipe", "dp"))
    chips = size // 2
    reach = chips // 4
    v, q, k = rows_in[0, 0], queries[0, 0], keys[0, 0]
    beta, gate, ids = strengths[0, 0], gates[0, 0], doc_ids[0]
    core = (lax.axis_index("ctx") % 2).astype(jnp.int32).reshape(1)

    def swapped(x):
        return lax.ppermute(x, "ctx", [(i, i ^ 1) for i in range(size)])

    def from_behind(x, d):
        return lax.ppermute(x, "ctx", [(i, i + 2 * d) for i in range(size - 2 * d)])

    big = (heads * SUB + META, SUB)
    send, keep, wv, yy, p0, u0, k, v, beta, gate, ids = call(
        functools.partial(chunk_kernel, heads, subs),
        [(big, BF16), (big, BF16), ((length, width), F32), ((length, width), BF16)]
        + [((heads * SUB, SUB), BF16)] * 2 + [((length, width), BF16)] * 2
        + [((heads, length), F32)] * 2 + [((1, length), jnp.int32)],
        "chunks", [SMEM] + [HBM] * 5, 1 << 31,
        [pltpu.SemaphoreType.DMA((3 + 2 * subs,))],
    )(core, *(pltpu.with_memory_space_constraint(x, pltpu.HBM) for x in (k, v, beta, gate, ids)))
    got = swapped(send)
    full, tail = call(
        functools.partial(pair_kernel, heads),
        [(big, BF16), ((half * SUB + META, SUB), BF16)],
        "pair", [SMEM, VMEM, VMEM], 1 << 25,
    )(core, keep, got)
    arrived = [from_behind(full, d) for d in range(1, reach)] + [from_behind(tail, reach)]
    local, reached, gain, pos = call(
        functools.partial(query_kernel, heads, subs),
        [((length, width), F32), ((length, width), BF16), (norm_gain.shape, F32), ((1, ndoc), jnp.int32)],
        "queries", [VMEM] * 11, 1 << 31,
    )(q, k, beta, gate, ids, wv, yy, p0, u0, norm_gain, positives[0])
    arrived, local, reached, gain, pos = lax.optimization_barrier((arrived, local, reached, gain, pos))
    give, mine = call(
        functools.partial(enter_kernel, heads, reach),
        [((half * SUB, SUB), BF16)] * 2,
        "enter", [SMEM] + [VMEM] * (2 + reach), 1 << 25,
    )(core, keep, got, *arrived)
    theirs = swapped(give)
    outs = [((length, width), BF16), ((ndoc, width), BF16)]
    rest = (local, reached, v, gain, ids)
    begun = call(
        functools.partial(rows_kernel, heads, ndoc, True), outs, "rows_own", [SMEM] + [VMEM] * 6, 1 << 31
    )(core, mine, *rest)
    rows_out, pooled = call(
        functools.partial(rows_kernel, heads, ndoc, False), outs, "rows_other",
        [SMEM] + [VMEM] * 8, 1 << 26, aliases={7: 0, 8: 1},
    )(core, theirs, *rest, *begun)
    passed = lax.ppermute(rows_out, "pipe", [(i, (i + 1) % pipes) for i in range(pipes)])
    (sums,) = call(add_kernel, [((chips, ndoc, width), BF16)], "sums", [VMEM, VMEM])(pooled, swapped(pooled))
    sides = [list(range(i, size, 2)) for i in range(2)]
    parts = lax.all_to_all(sums, "ctx", 0, 0, axis_index_groups=sides)
    if replicas == 1:
        loss, passed = pl.pallas_call(
            final_kernel,
            out_shape=[pltpu.HBM((1, ndoc), F32), pltpu.HBM(passed.shape, passed.dtype)],
            in_specs=[VMEM] * 3,
            out_specs=[HBM, HBM],
            scratch_shapes=[
                pltpu.VMEM((1, ndoc), F32), pltpu.SemaphoreType.DMA((8,)), pltpu.SemaphoreType.DMA
            ],
            compiler_params=pltpu.CompilerParams(vmem_limit_bytes=40 << 20),
            name="final",
        )(parts, pos, passed)
    else:
        mine = unit(jnp.sum(parts.astype(F32), axis=0))
        cands = lax.all_gather(mine.astype(BF16), "dp", axis=0, tiled=True).astype(F32)
        loss = losses(dot(cands, mine, NT, HIGHEST) / 0.05, lax.axis_index("dp") * ndoc, pos)
    return (passed.reshape(1, 1, length, width), loss.reshape(1, 1, ndoc))


def solution(mesh):
    rows = P(("groups", "pipe"), "dp", "ctx", None)
    tokens = P(("groups", "pipe"), "dp", None, "ctx")
    docs = P(("groups", "pipe"), "dp", None)
    in_specs = (
        rows, rows, rows, tokens, tokens, P(("groups", "pipe"), "dp", "ctx"), docs, P("pipe", None)
    )
    return jax.shard_map(
        on_device, mesh=mesh, in_specs=in_specs, out_specs=(rows, docs), check_vma=False
    )
```

```python
import functools

import jax
import jax.numpy as jnp
from jax import lax
from jax.experimental import pallas as pl
from jax.experimental.pallas import tpu as pltpu
from jax.sharding import PartitionSpec as P

F32, BF16 = jnp.float32, jnp.bfloat16
HIGHEST = lax.Precision.HIGHEST
NEG = -1e30
SUB = 128
META = 16

NN = (((1,), (0,)), ((), ()))
NT = (((1,), (1,)), ((), ()))
TN = (((0,), (0,)), ((), ()))


def dot(a, b, dims=NN, precision=None):
    return lax.dot_general(a, b, dims, precision=precision, preferred_element_type=F32)


def dot1(a, b, dims=NN):
    return dot(a.astype(BF16), b.astype(BF16), dims)


def split(x):
    high = x.astype(BF16)
    return high, (x - high.astype(F32)).astype(BF16)


def dot3(a, b, dims=NN):
    (ah, al), (bh, bl) = split(a), split(b)
    return dot(ah, bh, dims) + (dot(al, bh, dims) + dot(ah, bl, dims))


def unit(x):
    return x * lax.rsqrt(jnp.sum(x * x, axis=-1, keepdims=True) + 1e-06)


def iotas():
    shape = (SUB, SUB)
    return lax.broadcasted_iota(jnp.int32, shape, 0), lax.broadcasted_iota(jnp.int32, shape, 1)


def per_token(rows, heads, subs):
    return jnp.concatenate([rows[:, j * SUB : (j + 1) * SUB] for j in range(subs)], axis=0)


class Decay:
    def __init__(self, gates, ids, heads, subs):
        r, c = iotas()
        upto = (c <= r).astype(F32)
        logs = per_token(jnp.log(gates), heads, subs)
        self.row = dot(logs, upto, NT, HIGHEST)
        self.col = dot(upto, logs, NT, HIGHEST)
        ids = ids.astype(F32)
        self.eye = (r == c).astype(F32)
        self.id_row = [ids[:, j * SUB : (j + 1) * SUB] for j in range(subs)]
        stacked = jnp.concatenate([jnp.broadcast_to(x, (8, SUB)) for x in self.id_row], axis=0)
        turned = dot1(self.eye, stacked, NT)
        self.id_col = [turned[:, 8 * j : 8 * j + 1] for j in range(subs)]
        self.heads, self.r, self.c = heads, r, c
        lead, tail = [], []
        for j in range(subs):
            row, last = self.row[j * heads : (j + 1) * heads], self.id_row[j][:, SUB - 1 :]
            entry = self.id_row[0][:, :1] if j == 0 else self.id_row[j - 1][:, SUB - 1 :]
            lead.append(jnp.where(self.id_row[j] == entry, jnp.exp(row), 0.0))
            tail.append(jnp.exp(jnp.where(self.id_row[j] == last, row[:, SUB - 1 :] - row, NEG)))
        self.lead = jnp.concatenate(lead, axis=0)
        self.tail = jnp.concatenate(tail, axis=0)
        self.same = [(x == y) & (r >= c) for x, y in zip(self.id_col, self.id_row)]

    def inner(self, h, j, keep):
        i = j * self.heads + h
        return jnp.exp(jnp.where(keep[j], self.col[:, i : i + 1] - self.row[i : i + 1, :], NEG))


def block(ref, h, j):
    return ref[j * SUB : (j + 1) * SUB, h * SUB : (h + 1) * SUB]


def chunk_kernel(
    heads, subs, core_ref, k_hbm, v_hbm, beta_hbm, gates_hbm, ids_hbm,
    send_ref, keep_ref, wv_ref, yy_ref, p0_ref, u0_ref, k_ref, v_ref,
    beta_ref, gates_ref, ids_ref, sems,
):
    small = [(gates_hbm, gates_ref), (ids_hbm, ids_ref), (beta_hbm, beta_ref)]
    parts = [pl.ds(j * SUB, SUB) for j in range(subs)]
    large = [(x.at[p, :], y.at[p, :]) for x, y in ((k_hbm, k_ref), (v_hbm, v_ref)) for p in parts]
    copies = [pltpu.make_async_copy(x, y, sems.at[i]) for i, (x, y) in enumerate(small + large)]
    for copy in copies:
        copy.start()
    for copy in copies[:3]:
        copy.wait()
    decay = Decay(gates_ref[...], ids_ref[...], heads, subs)
    r, c, eye = decay.r, decay.c, decay.eye
    beta = per_token(beta_ref[...], heads, subs)
    tails = decay.tail * beta
    strict = [x & (r > c) for x in decay.same]
    chains = [(h, j) for j in range(subs) for h in range(heads)]
    kn, kt, low, inv = {}, {}, {}, {}
    for h, j in chains:
        if h == 0:
            copies[3 + j].wait()
        unit_keys = unit(block(k_ref, h, j).astype(F32))
        kn[h, j] = unit_keys.astype(BF16)
        kt[h, j] = unit_keys.T
    near = ((r // 2) == (c // 2)) & (r > c)
    for h, j in chains:
        i = j * heads + h
        gram = dot(kn[h, j], kt[h, j].astype(BF16))
        full = decay.inner(h, j, strict) * gram * beta[i : i + 1, :]
        inv[h, j] = eye - jnp.where(near, full, 0.0)
        low[h, j] = full.astype(BF16)
    size = 2
    while size < SUB:
        pick = (((r // size) % 2 == 1) & ((c // size) == (r // size) - 1)).astype(BF16)
        odd = range(size, SUB, 2 * size)
        half, rows = {}, {}
        for key in chains:
            rows[key] = inv[key]
            if size >= 8:
                rows[key] = jnp.concatenate([inv[key][o : o + size] for o in odd], axis=0)
            half[key] = dot1(rows[key], low[key] * pick)
        for key in chains:
            new = rows[key] - dot1(half[key], inv[key])
            if size >= 8:
                parts = []
                for n, o in enumerate(odd):
                    parts += [inv[key][o - size : o], new[n * size : (n + 1) * size]]
                new = jnp.concatenate(parts, axis=0)
            inv[key] = new
        size *= 2
    for copy in copies[3 + subs :]:
        copy.wait()
    wv, yy, pp, uu = {}, {}, {}, {}
    for h, j in chains:
        i = j * heads + h
        xh, xl = split(inv[h, j])
        values = block(v_ref, h, j)
        wv[h, j] = dot(xh, values) + dot(xl, values)
        yy[h, j] = dot((inv[h, j] * decay.lead[i : i + 1, :]).astype(BF16), kn[h, j]).astype(BF16)
        wv_ref[j * SUB : (j + 1) * SUB, h * SUB : (h + 1) * SUB] = wv[h, j]
        yy_ref[j * SUB : (j + 1) * SUB, h * SUB : (h + 1) * SUB] = yy[h, j]
    for h, j in chains:
        i = j * heads + h
        dh, dl = split(kt[h, j] * tails[i : i + 1, :])
        wh, wl = split(wv[h, j])
        got = dot(dh, jnp.concatenate([wh, yy[h, j]], axis=1))
        pp[h, j] = decay.lead[i : i + 1, SUB - 1 :] * eye - got[:, SUB:]
        uu[h, j] = got[:, :SUB] + (dot(dl, wh) + dot(dh, wl))
    for h in range(heads):
        p0, u0 = pp[h, 0].astype(BF16), uu[h, 0].astype(BF16)
        p0_ref[h * SUB : (h + 1) * SUB, :] = p0
        u0_ref[h * SUB : (h + 1) * SUB, :] = u0
        for j in range(1, subs):
            got = dot1(pp[h, j], jnp.concatenate([u0, p0], axis=1))
            uu[h, 0] = uu[h, j] + got[:, :SUB]
            pp[h, 0] = got[:, SUB:]
            u0, p0 = uu[h, 0].astype(BF16), pp[h, 0].astype(BF16)
    half_heads = heads // 2
    first = core_ref[0] == 0
    for h in range(half_heads):
        for base, part in ((0, pp), (half_heads, uu)):
            lo, hi = part[h, 0].astype(BF16), part[half_heads + h, 0].astype(BF16)
            at = slice((base + h) * SUB, (base + h + 1) * SUB)
            send_ref[at, :] = jnp.where(first, hi, lo)
            keep_ref[at, :] = jnp.where(first, lo, hi)
    start = decay.id_row[0][:, :1]
    end = decay.id_row[-1][:, SUB - 1 :]
    which = lax.broadcasted_iota(jnp.int32, (META, SUB), 0) < META // 2
    meta = jnp.where(which, end, start).astype(BF16)
    send_ref[heads * SUB :, :] = meta
    keep_ref[heads * SUB :, :] = meta


def query_kernel(
    heads, subs, q_ref, k_ref, beta_ref, gates_ref, ids_ref, wv_ref, yy_ref, p0_ref, u0_ref,
    gain_in, pos_in, local_ref, reach_ref, gain_ref, pos_ref,
):
    gain_ref[...] = gain_in[...]
    pos_ref[...] = pos_in[...]
    decay = Decay(gates_ref[...], ids_ref[...], heads, subs)
    beta = per_token(beta_ref[...], heads, subs)
    lead = dot(decay.eye, decay.lead, NT, HIGHEST)
    chains = [(h, j) for j in range(subs) for h in range(heads)]
    qn, attend, reach, local = {}, {}, {}, {}
    for h, j in chains:
        i = j * heads + h
        qn[h, j] = unit(block(q_ref, h, j).astype(F32))
        kn = unit(block(k_ref, h, j).astype(F32))
        attend[h, j] = decay.inner(h, j, decay.same) * dot3(qn[h, j], kn, NT) * beta[i : i + 1, :]
    for h, j in chains:
        i = j * heads + h
        ah, al = split(attend[h, j])
        wh, wl = split(block(wv_ref, h, j))
        reach[h, j] = lead[:, i : i + 1] * qn[h, j] - dot(ah, block(yy_ref, h, j))
        local[h, j] = dot(ah, wh) + (dot(al, wh) + dot(ah, wl))
    for h, j in chains:
        if j > 0:
            rb = reach[h, j].astype(BF16)
            at = slice(h * SUB, (h + 1) * SUB)
            local[h, j] = local[h, j] + dot(rb, u0_ref[at, :])
            reach[h, j] = dot(rb, p0_ref[at, :])
        local_ref[j * SUB : (j + 1) * SUB, h * SUB : (h + 1) * SUB] = local[h, j]
        reach_ref[j * SUB : (j + 1) * SUB, h * SUB : (h + 1) * SUB] = reach[h, j].astype(BF16)


def ends(ref, rows):
    meta = ref[rows : rows + META, :].astype(F32)
    return meta[META // 2 : META // 2 + 1, :], meta[:1, :]


def pair_kernel(heads, core_ref, keep_ref, got_ref, full_ref, tail_ref):
    half = heads // 2
    first = core_ref[0] == 0
    own, other = ends(keep_ref, heads * SUB), ends(got_ref, heads * SUB)
    early = [jnp.where(first, a, b) for a, b in zip(own, other)]
    late = [jnp.where(first, b, a) for a, b in zip(own, other)]
    joined = (early[1] == late[0]).astype(F32)
    for h in range(half):
        at, up = slice(h * SUB, (h + 1) * SUB), slice((half + h) * SUB, (half + h + 1) * SUB)
        p1 = jnp.where(first, keep_ref[at, :], got_ref[at, :])
        p2 = jnp.where(first, got_ref[at, :], keep_ref[at, :])
        u1 = jnp.where(first, keep_ref[up, :], got_ref[up, :])
        u2 = jnp.where(first, got_ref[up, :], keep_ref[up, :])
        full_ref[at, :] = (joined * dot(p2, p1)).astype(BF16)
        state = (u2.astype(F32) + joined * dot(p2, u1)).astype(BF16)
        full_ref[up, :] = state
        tail_ref[at, :] = state
    which = lax.broadcasted_iota(jnp.int32, (META, SUB), 0) < META // 2
    meta = jnp.where(which, late[1], early[0]).astype(BF16)
    full_ref[heads * SUB :, :] = meta
    tail_ref[half * SUB :, :] = meta


def enter_kernel(heads, reach, core_ref, keep_ref, got_ref, *refs):
    chips, (send_ref, mine_ref) = refs[:reach], refs[reach:]
    half = heads // 2
    first = core_ref[0] == 0
    own, other = ends(keep_ref, heads * SUB), ends(got_ref, heads * SUB)
    early = [jnp.where(first, a, b) for a, b in zip(own, other)]
    late = [jnp.where(first, b, a) for a, b in zip(own, other)]
    marks = [(early[0], None)]
    for d, ref in enumerate(chips):
        marks.append(ends(ref, (heads if d < reach - 1 else half) * SUB))
    links = [(marks[d][0] == marks[d + 1][1]).astype(F32) for d in range(reach)]
    joined = (early[1] == late[0]).astype(F32)
    ats = [slice(h * SUB, (h + 1) * SUB) for h in range(half)]
    ups = [slice((half + h) * SUB, (half + h + 1) * SUB) for h in range(half)]
    states = [chips[-1][at, :].astype(F32) for at in ats]
    for d in range(reach - 2, -1, -1):
        moved = [dot1(chips[d][at, :], state) for at, state in zip(ats, states)]
        states = [chips[d][up, :].astype(F32) + links[d + 1] * x for up, x in zip(ups, moved)]
    states = [(links[0] * state).astype(BF16) for state in states]
    moved = [
        dot(jnp.where(first, keep_ref[at, :], got_ref[at, :]), state) for at, state in zip(ats, states)
    ]
    for at, up, state, x in zip(ats, ups, states, moved):
        u1 = jnp.where(first, keep_ref[up, :], got_ref[up, :])
        middle = (joined * (u1.astype(F32) + x)).astype(BF16)
        send_ref[at, :] = jnp.where(first, middle, state)
        mine_ref[at, :] = jnp.where(first, state, middle)


def rows_kernel(
    heads, ndoc, own, core_ref, state_ref, local_ref, reach_ref, v_ref, gain_ref, ids_ref, *refs
):
    out_ref, pooled_ref = refs[-2:]
    half = heads // 2
    group = core_ref[0] if own else 1 - core_ref[0]
    docs = lax.broadcasted_iota(jnp.int32, (ndoc, v_ref.shape[0]), 0)
    onehot = (docs == ids_ref[...]).astype(F32).astype(BF16)
    gain = gain_ref[...]
    mean = jnp.full((SUB, SUB), 1.0 / SUB, BF16)
    cols = [pl.ds(pl.multiple_of((group * half + h) * SUB, SUB), SUB) for h in range(half)]
    outs = [
        local_ref[:, x] + dot(reach_ref[:, x], state_ref[h * SUB : (h + 1) * SUB, :])
        for h, x in enumerate(cols)
    ]
    scales = [lax.rsqrt(dot1(o * o, mean) + 1e-06) * gain for o in outs]
    outs = [
        (v_ref[:, x].astype(F32) + o * scale).astype(BF16) for x, o, scale in zip(cols, outs, scales)
    ]
    sums = [dot(onehot, out).astype(BF16) for out in outs]
    for x, out, pooled in zip(cols, outs, sums):
        out_ref[:, x] = out
        pooled_ref[:, x] = pooled


def losses(scores, own, pos):
    cidx = lax.broadcasted_iota(jnp.int32, scores.shape, 0)
    didx = lax.broadcasted_iota(jnp.int32, scores.shape, 1)
    total = jnp.sum(jnp.where(cidx != own + didx, jnp.exp(scores), 0.0), axis=0, keepdims=True)
    picked = jnp.sum(jnp.where(cidx == pos, scores, 0.0), axis=0, keepdims=True)
    return jnp.log(total) - picked


def add_kernel(a_ref, b_ref, out_ref):
    total = (a_ref[...].astype(F32) + b_ref[...].astype(F32)).astype(BF16)
    for i in range(out_ref.shape[0]):
        out_ref[i] = total


def store_rows(rows_ref, out_ref, sems):
    pieces = sems.shape[0]
    step = rows_ref.shape[0] // pieces
    at = [pl.ds(i * step, step) for i in range(pieces)]
    return [pltpu.make_async_copy(rows_ref.at[x, :], out_ref.at[x, :], sems.at[i]) for i, x in enumerate(at)]


def final_kernel(parts_ref, pos_ref, rows_ref, loss_out, out_ref, loss_ref, sems, loss_sem):
    copies = store_rows(rows_ref, out_ref, sems)
    for copy in copies:
        copy.start()
    sums = jnp.sum(parts_ref[...].astype(F32), axis=0)
    gram = dot(sums, sums, NT, HIGHEST)
    cidx = lax.broadcasted_iota(jnp.int32, gram.shape, 0)
    didx = lax.broadcasted_iota(jnp.int32, gram.shape, 1)
    squares = jnp.where(cidx == didx, gram, 0.0)
    across = lax.rsqrt(jnp.sum(squares, axis=0, keepdims=True) + 1e-06)
    down = lax.rsqrt(jnp.sum(squares, axis=1, keepdims=True) + 1e-06)
    loss_ref[...] = losses(gram * across * down / 0.05, 0, pos_ref[...])
    copies.append(pltpu.make_async_copy(loss_ref, loss_out, loss_sem))
    copies[-1].start()
    for copy in copies:
        copy.wait()


VMEM = pl.BlockSpec(memory_space=pltpu.VMEM)
SMEM = pl.BlockSpec(memory_space=pltpu.SMEM)
HBM = pl.BlockSpec(memory_space=pltpu.HBM)


def call(body, outs, name, specs, flops=0, scratch=(), aliases={}):
    return pl.pallas_call(
        body,
        out_shape=[jax.ShapeDtypeStruct(s, d) for s, d in outs],
        in_specs=specs,
        out_specs=[VMEM] * len(outs),
        scratch_shapes=scratch,
        input_output_aliases=aliases,
        compiler_params=pltpu.CompilerParams(vmem_limit_bytes=40 << 20),
        cost_estimate=pl.CostEstimate(flops=flops, bytes_accessed=4 << 20, transcendentals=0),
        name=name,
    )


def on_device(rows_in, queries, keys, strengths, gates, doc_ids, positives, norm_gain):
    length, width = rows_in.shape[2], rows_in.shape[3]
    heads, ndoc = strengths.shape[2], positives.shape[2]
    subs = length // SUB
    half = heads // 2
    size, pipes, replicas = (lax.axis_size(x) for x in ("ctx", "pipe", "dp"))
    chips = size // 2
    reach = chips // 4
    v, q, k = rows_in[0, 0], queries[0, 0], keys[0, 0]
    beta, gate, ids = strengths[0, 0], gates[0, 0], doc_ids[0]
    core = (lax.axis_index("ctx") % 2).astype(jnp.int32).reshape(1)

    def swapped(x):
        return lax.ppermute(x, "ctx", [(i, i ^ 1) for i in range(size)])

    def from_behind(x, d):
        return lax.ppermute(x, "ctx", [(i, i + 2 * d) for i in range(size - 2 * d)])

    big = (heads * SUB + META, SUB)
    send, keep, wv, yy, p0, u0, k, v, beta, gate, ids = call(
        functools.partial(chunk_kernel, heads, subs),
        [(big, BF16), (big, BF16), ((length, width), F32), ((length, width), BF16)]
        + [((heads * SUB, SUB), BF16)] * 2 + [((length, width), BF16)] * 2
        + [((heads, length), F32)] * 2 + [((1, length), jnp.int32)],
        "chunks", [SMEM] + [HBM] * 5, 1 << 31,
        [pltpu.SemaphoreType.DMA((3 + 2 * subs,))],
    )(core, *(pltpu.with_memory_space_constraint(x, pltpu.HBM) for x in (k, v, beta, gate, ids)))
    got = swapped(send)
    full, tail = call(
        functools.partial(pair_kernel, heads),
        [(big, BF16), ((half * SUB + META, SUB), BF16)],
        "pair", [SMEM, VMEM, VMEM], 1 << 25,
    )(core, keep, got)
    arrived = [from_behind(full, d) for d in range(1, reach)] + [from_behind(tail, reach)]
    local, reached, gain, pos = call(
        functools.partial(query_kernel, heads, subs),
        [((length, width), F32), ((length, width), BF16), (norm_gain.shape, F32), ((1, ndoc), jnp.int32)],
        "queries", [VMEM] * 11, 1 << 31,
    )(q, k, beta, gate, ids, wv, yy, p0, u0, norm_gain, positives[0])
    arrived, local, reached, gain, pos = lax.optimization_barrier((arrived, local, reached, gain, pos))
    give, mine = call(
        functools.partial(enter_kernel, heads, reach),
        [((half * SUB, SUB), BF16)] * 2,
        "enter", [SMEM] + [VMEM] * (2 + reach), 1 << 25,
    )(core, keep, got, *arrived)
    theirs = swapped(give)
    outs = [((length, width), BF16), ((ndoc, width), BF16)]
    rest = (local, reached, v, gain, ids)
    begun = call(
        functools.partial(rows_kernel, heads, ndoc, True), outs, "rows_own", [SMEM] + [VMEM] * 6, 1 << 31
    )(core, mine, *rest)
    rows_out, pooled = call(
        functools.partial(rows_kernel, heads, ndoc, False), outs, "rows_other",
        [SMEM] + [VMEM] * 8, 1 << 26, aliases={7: 0, 8: 1},
    )(core, theirs, *rest, *begun)
    passed = lax.ppermute(rows_out, "pipe", [(i, (i + 1) % pipes) for i in range(pipes)])
    (sums,) = call(add_kernel, [((chips, ndoc, width), BF16)], "sums", [VMEM, VMEM])(pooled, swapped(pooled))
    sides = [list(range(i, size, 2)) for i in range(2)]
    parts = lax.all_to_all(sums, "ctx", 0, 0, axis_index_groups=sides)
    if replicas == 1:
        loss, passed = pl.pallas_call(
            final_kernel,
            out_shape=[pltpu.HBM((1, ndoc), F32), pltpu.HBM(passed.shape, passed.dtype)],
            in_specs=[VMEM] * 3,
            out_specs=[HBM, HBM],
            scratch_shapes=[
                pltpu.VMEM((1, ndoc), F32), pltpu.SemaphoreType.DMA((8,)), pltpu.SemaphoreType.DMA
            ],
            compiler_params=pltpu.CompilerParams(vmem_limit_bytes=40 << 20),
            name="final",
        )(parts, pos, passed)
    else:
        mine = unit(jnp.sum(parts.astype(F32), axis=0))
        cands = lax.all_gather(mine.astype(BF16), "dp", axis=0, tiled=True).astype(F32)
        loss = losses(dot(cands, mine, NT, HIGHEST) / 0.05, lax.axis_index("dp") * ndoc, pos)
    return (passed.reshape(1, 1, length, width), loss.reshape(1, 1, ndoc))


def solution(mesh):
    rows = P(("groups", "pipe"), "dp", "ctx", None)
    tokens = P(("groups", "pipe"), "dp", None, "ctx")
    docs = P(("groups", "pipe"), "dp", None)
    in_specs = (
        rows, rows, rows, tokens, tokens, P(("groups", "pipe"), "dp", "ctx"), docs, P("pipe", None)
    )
    return jax.shard_map(
        on_device, mesh=mesh, in_specs=in_specs, out_specs=(rows, docs), check_vma=False
    )
```

```python
import functools

import jax
import jax.numpy as jnp
from jax import lax
from jax.experimental import pallas as pl
from jax.experimental.pallas import tpu as pltpu
from jax.sharding import PartitionSpec as P

F32, BF16 = jnp.float32, jnp.bfloat16
HIGHEST = lax.Precision.HIGHEST
NEG = -1e30
SUB = 128
META = 16

NN = (((1,), (0,)), ((), ()))
NT = (((1,), (1,)), ((), ()))
TN = (((0,), (0,)), ((), ()))


def dot(a, b, dims=NN, precision=None):
    return lax.dot_general(a, b, dims, precision=precision, preferred_element_type=F32)


def dot1(a, b, dims=NN):
    return dot(a.astype(BF16), b.astype(BF16), dims)


def split(x):
    high = x.astype(BF16)
    return high, (x - high.astype(F32)).astype(BF16)


def dot3(a, b, dims=NN):
    (ah, al), (bh, bl) = split(a), split(b)
    return dot(ah, bh, dims) + (dot(al, bh, dims) + dot(ah, bl, dims))


def dot2(a, b):
    high, low = split(b)
    return dot(a, high) + dot(a, low)


def unit(x):
    return x * lax.rsqrt(jnp.sum(x * x, axis=-1, keepdims=True) + 1e-06)


def iotas():
    shape = (SUB, SUB)
    return lax.broadcasted_iota(jnp.int32, shape, 0), lax.broadcasted_iota(jnp.int32, shape, 1)


def per_token(rows, heads, subs):
    return jnp.concatenate([rows[:, j * SUB : (j + 1) * SUB] for j in range(subs)], axis=0)


class Decay:
    def __init__(self, gates, ids, heads, subs):
        r, c = iotas()
        upto = (c <= r).astype(F32)
        logs = per_token(jnp.log(gates), heads, subs)
        self.row = dot(logs, upto, NT, HIGHEST)
        self.col = dot(upto, logs, NT, HIGHEST)
        ids = ids.astype(F32)
        self.eye = (r == c).astype(F32)
        self.id_row = [ids[:, j * SUB : (j + 1) * SUB] for j in range(subs)]
        stacked = jnp.concatenate([jnp.broadcast_to(x, (8, SUB)) for x in self.id_row], axis=0)
        turned = dot1(self.eye, stacked, NT)
        self.id_col = [turned[:, 8 * j : 8 * j + 1] for j in range(subs)]
        self.heads, self.r, self.c = heads, r, c
        lead, tail = [], []
        for j in range(subs):
            row, last = self.row[j * heads : (j + 1) * heads], self.id_row[j][:, SUB - 1 :]
            entry = self.id_row[0][:, :1] if j == 0 else self.id_row[j - 1][:, SUB - 1 :]
            lead.append(jnp.where(self.id_row[j] == entry, jnp.exp(row), 0.0))
            tail.append(jnp.exp(jnp.where(self.id_row[j] == last, row[:, SUB - 1 :] - row, NEG)))
        self.lead = jnp.concatenate(lead, axis=0)
        self.tail = jnp.concatenate(tail, axis=0)
        self.same = [(x == y) & (r >= c) for x, y in zip(self.id_col, self.id_row)]

    def inner(self, h, j, keep):
        i = j * self.heads + h
        return jnp.exp(jnp.where(keep[j], self.col[:, i : i + 1] - self.row[i : i + 1, :], NEG))


def block(ref, h, j):
    return ref[j * SUB : (j + 1) * SUB, h * SUB : (h + 1) * SUB]


def chunk_kernel(
    heads, subs, core_ref, k_hbm, v_hbm, beta_hbm, gates_hbm, ids_hbm,
    send_ref, keep_ref, wv_ref, yy_ref, p0_ref, u0_ref, k_ref, v_ref,
    beta_ref, gates_ref, ids_ref, sems,
):
    small = [(gates_hbm, gates_ref), (ids_hbm, ids_ref), (beta_hbm, beta_ref)]
    parts = [pl.ds(j * SUB, SUB) for j in range(subs)]
    large = [(x.at[p, :], y.at[p, :]) for x, y in ((k_hbm, k_ref), (v_hbm, v_ref)) for p in parts]
    copies = [pltpu.make_async_copy(x, y, sems.at[i]) for i, (x, y) in enumerate(small + large)]
    for copy in copies:
        copy.start()
    for copy in copies[:3]:
        copy.wait()
    decay = Decay(gates_ref[...], ids_ref[...], heads, subs)
    r, c, eye = decay.r, decay.c, decay.eye
    beta = per_token(beta_ref[...], heads, subs)
    tails = decay.tail * beta
    strict = [x & (r > c) for x in decay.same]
    chains = [(h, j) for j in range(subs) for h in range(heads)]
    kn, kt, low, inv = {}, {}, {}, {}
    for h, j in chains:
        if h == 0:
            copies[3 + j].wait()
        unit_keys = unit(block(k_ref, h, j).astype(F32))
        kn[h, j] = unit_keys.astype(BF16)
        kt[h, j] = unit_keys.T
    near = ((r // 2) == (c // 2)) & (r > c)
    for h, j in chains:
        i = j * heads + h
        gram = dot(kn[h, j], kt[h, j].astype(BF16))
        full = decay.inner(h, j, strict) * gram * beta[i : i + 1, :]
        inv[h, j] = eye - jnp.where(near, full, 0.0)
        low[h, j] = full.astype(BF16)
    size = 2
    while size < SUB:
        pick = (((r // size) % 2 == 1) & ((c // size) == (r // size) - 1)).astype(BF16)
        odd = range(size, SUB, 2 * size)
        half, rows = {}, {}
        for key in chains:
            rows[key] = inv[key]
            if size >= 8:
                rows[key] = jnp.concatenate([inv[key][o : o + size] for o in odd], axis=0)
            half[key] = dot1(rows[key], low[key] * pick)
        for key in chains:
            new = rows[key] - dot1(half[key], inv[key])
            if size >= 8:
                parts = []
                for n, o in enumerate(odd):
                    parts += [inv[key][o - size : o], new[n * size : (n + 1) * size]]
                new = jnp.concatenate(parts, axis=0)
            inv[key] = new
        size *= 2
    for copy in copies[3 + subs :]:
        copy.wait()
    wv, yy, pp, uu = {}, {}, {}, {}
    for h, j in chains:
        i = j * heads + h
        xh, xl = split(inv[h, j])
        values = block(v_ref, h, j)
        wv[h, j] = dot(xh, values) + dot(xl, values)
        yy[h, j] = dot((inv[h, j] * decay.lead[i : i + 1, :]).astype(BF16), kn[h, j]).astype(BF16)
        wv_ref[j * SUB : (j + 1) * SUB, h * SUB : (h + 1) * SUB] = wv[h, j]
        yy_ref[j * SUB : (j + 1) * SUB, h * SUB : (h + 1) * SUB] = yy[h, j]
    for h, j in chains:
        i = j * heads + h
        dh, dl = split(kt[h, j] * tails[i : i + 1, :])
        wh, wl = split(wv[h, j])
        got = dot(dh, jnp.concatenate([wh, yy[h, j]], axis=1))
        pp[h, j] = decay.lead[i : i + 1, SUB - 1 :] * eye - got[:, SUB:]
        uu[h, j] = got[:, :SUB] + (dot(dl, wh) + dot(dh, wl))
    for h in range(heads):
        p0_ref[h * SUB : (h + 1) * SUB, :] = pp[h, 0]
        u0_ref[h * SUB : (h + 1) * SUB, :] = uu[h, 0]
    for j in range(1, subs):
        for h in range(heads):
            got = dot2(pp[h, j].astype(BF16), jnp.concatenate([uu[h, 0], pp[h, 0]], axis=1))
            uu[h, 0] = uu[h, j] + got[:, :SUB]
            pp[h, 0] = got[:, SUB:]
    half_heads = heads // 2
    first = core_ref[0] == 0
    for h in range(half_heads):
        for base, part in ((0, pp), (half_heads, uu)):
            lo, hi = part[h, 0].astype(BF16), part[half_heads + h, 0].astype(BF16)
            at = slice((base + h) * SUB, (base + h + 1) * SUB)
            send_ref[at, :] = jnp.where(first, hi, lo)
            keep_ref[at, :] = jnp.where(first, lo, hi)
    start = decay.id_row[0][:, :1]
    end = decay.id_row[-1][:, SUB - 1 :]
    which = lax.broadcasted_iota(jnp.int32, (META, SUB), 0) < META // 2
    meta = jnp.where(which, end, start).astype(BF16)
    send_ref[heads * SUB :, :] = meta
    keep_ref[heads * SUB :, :] = meta


def query_kernel(
    heads, subs, q_ref, k_ref, beta_ref, gates_ref, ids_ref, wv_ref, yy_ref, p0_ref, u0_ref,
    gain_in, pos_in, local_ref, reach_ref, gain_ref, pos_ref,
):
    gain_ref[...] = gain_in[...]
    pos_ref[...] = pos_in[...]
    decay = Decay(gates_ref[...], ids_ref[...], heads, subs)
    beta = per_token(beta_ref[...], heads, subs)
    lead = dot(decay.eye, decay.lead, NT, HIGHEST)
    chains = [(h, j) for j in range(subs) for h in range(heads)]
    qn, attend, reach, local = {}, {}, {}, {}
    for h, j in chains:
        i = j * heads + h
        qn[h, j] = unit(block(q_ref, h, j).astype(F32))
        kn = unit(block(k_ref, h, j).astype(F32))
        attend[h, j] = decay.inner(h, j, decay.same) * dot3(qn[h, j], kn, NT) * beta[i : i + 1, :]
    for h, j in chains:
        i = j * heads + h
        ah, al = split(attend[h, j])
        wh, wl = split(block(wv_ref, h, j))
        reach[h, j] = lead[:, i : i + 1] * qn[h, j] - dot(ah, block(yy_ref, h, j))
        local[h, j] = dot(ah, wh) + (dot(al, wh) + dot(ah, wl))
    for h, j in chains:
        if j > 0:
            at = slice(h * SUB, (h + 1) * SUB)
            got = dot3(reach[h, j], jnp.concatenate([u0_ref[at, :], p0_ref[at, :]], axis=1))
            local[h, j] = local[h, j] + got[:, :SUB]
            reach[h, j] = got[:, SUB:]
    for h, j in chains:
        rows, cols = slice(j * SUB, (j + 1) * SUB), slice(h * SUB, (h + 1) * SUB)
        local_ref[rows, cols] = local[h, j]
        reach_ref[0, rows, cols], reach_ref[1, rows, cols] = split(reach[h, j])


def ends(ref, rows):
    meta = ref[rows : rows + META, :].astype(F32)
    return meta[META // 2 : META // 2 + 1, :], meta[:1, :]


def pair_kernel(heads, core_ref, keep_ref, got_ref, full_ref, tail_ref):
    half = heads // 2
    first = core_ref[0] == 0
    own, other = ends(keep_ref, heads * SUB), ends(got_ref, heads * SUB)
    early = [jnp.where(first, a, b) for a, b in zip(own, other)]
    late = [jnp.where(first, b, a) for a, b in zip(own, other)]
    joined = (early[1] == late[0]).astype(F32)
    for h in range(half):
        at, up = slice(h * SUB, (h + 1) * SUB), slice((half + h) * SUB, (half + h + 1) * SUB)
        p1 = jnp.where(first, keep_ref[at, :], got_ref[at, :])
        p2 = jnp.where(first, got_ref[at, :], keep_ref[at, :])
        u1 = jnp.where(first, keep_ref[up, :], got_ref[up, :])
        u2 = jnp.where(first, got_ref[up, :], keep_ref[up, :])
        full_ref[at, :] = (joined * dot(p2, p1)).astype(BF16)
        state = (u2.astype(F32) + joined * dot(p2, u1)).astype(BF16)
        full_ref[up, :] = state
        tail_ref[at, :] = state
    which = lax.broadcasted_iota(jnp.int32, (META, SUB), 0) < META // 2
    meta = jnp.where(which, late[1], early[0]).astype(BF16)
    full_ref[heads * SUB :, :] = meta
    tail_ref[half * SUB :, :] = meta


def enter_kernel(heads, reach, core_ref, keep_ref, got_ref, *refs):
    chips, (send_ref, mine_ref) = refs[:reach], refs[reach:]
    half = heads // 2
    first = core_ref[0] == 0
    own, other = ends(keep_ref, heads * SUB), ends(got_ref, heads * SUB)
    early = [jnp.where(first, a, b) for a, b in zip(own, other)]
    late = [jnp.where(first, b, a) for a, b in zip(own, other)]
    marks = [(early[0], None)]
    for d, ref in enumerate(chips):
        marks.append(ends(ref, (heads if d < reach - 1 else half) * SUB))
    links = [(marks[d][0] == marks[d + 1][1]).astype(F32) for d in range(reach)]
    joined = (early[1] == late[0]).astype(F32)
    ats = [slice(h * SUB, (h + 1) * SUB) for h in range(half)]
    ups = [slice((half + h) * SUB, (half + h + 1) * SUB) for h in range(half)]
    states = [chips[-1][at, :].astype(F32) for at in ats]
    for d in range(reach - 2, -1, -1):
        moved = [dot2(chips[d][at, :], state) for at, state in zip(ats, states)]
        states = [chips[d][up, :].astype(F32) + links[d + 1] * x for up, x in zip(ups, moved)]
    states = [links[0] * state for state in states]
    moved = [
        dot2(jnp.where(first, keep_ref[at, :], got_ref[at, :]), state) for at, state in zip(ats, states)
    ]
    for at, up, state, x in zip(ats, ups, states, moved):
        u1 = jnp.where(first, keep_ref[up, :], got_ref[up, :])
        middle = joined * (u1.astype(F32) + x)
        send_ref[at, :] = jnp.where(first, middle, state)
        mine_ref[at, :] = jnp.where(first, state, middle)


def rows_kernel(
    heads, ndoc, own, core_ref, state_ref, local_ref, reach_ref, v_ref, gain_ref, ids_ref, *refs
):
    out_ref, pooled_ref = refs[-2:]
    half = heads // 2
    group = core_ref[0] if own else 1 - core_ref[0]
    docs = lax.broadcasted_iota(jnp.int32, (ndoc, v_ref.shape[0]), 0)
    onehot = (docs == ids_ref[...]).astype(F32).astype(BF16)
    gain = gain_ref[...]
    mean = jnp.full((SUB, SUB), 1.0 / SUB, BF16)
    cols = [pl.ds(pl.multiple_of((group * half + h) * SUB, SUB), SUB) for h in range(half)]
    outs = []
    for h, x in enumerate(cols):
        high, low = split(state_ref[h * SUB : (h + 1) * SUB, :])
        near, rest = reach_ref[0, :, x], reach_ref[1, :, x]
        outs.append(local_ref[:, x] + (dot(near, high) + (dot(rest, high) + dot(near, low))))
    scales = [lax.rsqrt(dot1(o * o, mean) + 1e-06) * gain for o in outs]
    outs = [
        (v_ref[:, x].astype(F32) + o * scale).astype(BF16) for x, o, scale in zip(cols, outs, scales)
    ]
    sums = [dot(onehot, out).astype(BF16) for out in outs]
    for x, out, pooled in zip(cols, outs, sums):
        out_ref[:, x] = out
        pooled_ref[:, x] = pooled


def losses(scores, own, pos):
    cidx = lax.broadcasted_iota(jnp.int32, scores.shape, 0)
    didx = lax.broadcasted_iota(jnp.int32, scores.shape, 1)
    total = jnp.sum(jnp.where(cidx != own + didx, jnp.exp(scores), 0.0), axis=0, keepdims=True)
    picked = jnp.sum(jnp.where(cidx == pos, scores, 0.0), axis=0, keepdims=True)
    return jnp.log(total) - picked


def add_kernel(a_ref, b_ref, out_ref):
    total = (a_ref[...].astype(F32) + b_ref[...].astype(F32)).astype(BF16)
    for i in range(out_ref.shape[0]):
        out_ref[i] = total


def store_rows(rows_ref, out_ref, sems):
    pieces = sems.shape[0]
    step = rows_ref.shape[0] // pieces
    at = [pl.ds(i * step, step) for i in range(pieces)]
    return [pltpu.make_async_copy(rows_ref.at[x, :], out_ref.at[x, :], sems.at[i]) for i, x in enumerate(at)]


def final_kernel(parts_ref, pos_ref, rows_ref, loss_out, out_ref, loss_ref, sems, loss_sem):
    copies = store_rows(rows_ref, out_ref, sems)
    for copy in copies:
        copy.start()
    sums = jnp.sum(parts_ref[...].astype(F32), axis=0)
    gram = dot(sums, sums, NT, HIGHEST)
    cidx = lax.broadcasted_iota(jnp.int32, gram.shape, 0)
    didx = lax.broadcasted_iota(jnp.int32, gram.shape, 1)
    squares = jnp.where(cidx == didx, gram, 0.0)
    across = lax.rsqrt(jnp.sum(squares, axis=0, keepdims=True) + 1e-06)
    down = lax.rsqrt(jnp.sum(squares, axis=1, keepdims=True) + 1e-06)
    loss_ref[...] = losses(gram * across * down / 0.05, 0, pos_ref[...])
    copies.append(pltpu.make_async_copy(loss_ref, loss_out, loss_sem))
    copies[-1].start()
    for copy in copies:
        copy.wait()


VMEM = pl.BlockSpec(memory_space=pltpu.VMEM)
SMEM = pl.BlockSpec(memory_space=pltpu.SMEM)
HBM = pl.BlockSpec(memory_space=pltpu.HBM)


def call(body, outs, name, specs, flops=0, scratch=(), aliases={}):
    return pl.pallas_call(
        body,
        out_shape=[jax.ShapeDtypeStruct(s, d) for s, d in outs],
        in_specs=specs,
        out_specs=[VMEM] * len(outs),
        scratch_shapes=scratch,
        input_output_aliases=aliases,
        compiler_params=pltpu.CompilerParams(vmem_limit_bytes=40 << 20),
        cost_estimate=pl.CostEstimate(flops=flops, bytes_accessed=4 << 20, transcendentals=0),
        name=name,
    )


def on_device(rows_in, queries, keys, strengths, gates, doc_ids, positives, norm_gain):
    length, width = rows_in.shape[2], rows_in.shape[3]
    heads, ndoc = strengths.shape[2], positives.shape[2]
    subs = length // SUB
    half = heads // 2
    size, pipes, replicas = (lax.axis_size(x) for x in ("ctx", "pipe", "dp"))
    chips = size // 2
    reach = chips // 4
    v, q, k = rows_in[0, 0], queries[0, 0], keys[0, 0]
    beta, gate, ids = strengths[0, 0], gates[0, 0], doc_ids[0]
    core = (lax.axis_index("ctx") % 2).astype(jnp.int32).reshape(1)

    def swapped(x):
        return lax.ppermute(x, "ctx", [(i, i ^ 1) for i in range(size)])

    def from_behind(x, d):
        return lax.ppermute(x, "ctx", [(i, i + 2 * d) for i in range(size - 2 * d)])

    big = (heads * SUB + META, SUB)
    send, keep, wv, yy, p0, u0, k, v, beta, gate, ids = call(
        functools.partial(chunk_kernel, heads, subs),
        [(big, BF16), (big, BF16), ((length, width), F32), ((length, width), BF16)]
        + [((heads * SUB, SUB), F32)] * 2 + [((length, width), BF16)] * 2
        + [((heads, length), F32)] * 2 + [((1, length), jnp.int32)],
        "chunks", [SMEM] + [HBM] * 5, 1 << 31,
        [pltpu.SemaphoreType.DMA((3 + 2 * subs,))],
    )(core, *(pltpu.with_memory_space_constraint(x, pltpu.HBM) for x in (k, v, beta, gate, ids)))
    got = swapped(send)
    full, tail = call(
        functools.partial(pair_kernel, heads),
        [(big, BF16), ((half * SUB + META, SUB), BF16)],
        "pair", [SMEM, VMEM, VMEM], 1 << 25,
    )(core, keep, got)
    arrived = [from_behind(full, d) for d in range(1, reach)] + [from_behind(tail, reach)]
    local, reached, gain, pos = call(
        functools.partial(query_kernel, heads, subs),
        [((length, width), F32), ((2, length, width), BF16), (norm_gain.shape, F32), ((1, ndoc), jnp.int32)],
        "queries", [VMEM] * 11, 1 << 31,
    )(q, k, beta, gate, ids, wv, yy, p0, u0, norm_gain, positives[0])
    arrived, local, reached, gain, pos = lax.optimization_barrier((arrived, local, reached, gain, pos))
    give, mine = call(
        functools.partial(enter_kernel, heads, reach),
        [((half * SUB, SUB), F32)] * 2,
        "enter", [SMEM] + [VMEM] * (2 + reach), 1 << 25,
    )(core, keep, got, *arrived)
    theirs = swapped(give)
    outs = [((length, width), BF16), ((ndoc, width), BF16)]
    rest = (local, reached, v, gain, ids)
    begun = call(
        functools.partial(rows_kernel, heads, ndoc, True), outs, "rows_own", [SMEM] + [VMEM] * 6, 1 << 31
    )(core, mine, *rest)
    rows_out, pooled = call(
        functools.partial(rows_kernel, heads, ndoc, False), outs, "rows_other",
        [SMEM] + [VMEM] * 8, 1 << 26, aliases={7: 0, 8: 1},
    )(core, theirs, *rest, *begun)
    passed = lax.ppermute(rows_out, "pipe", [(i, (i + 1) % pipes) for i in range(pipes)])
    (sums,) = call(add_kernel, [((chips, ndoc, width), BF16)], "sums", [VMEM, VMEM])(pooled, swapped(pooled))
    sides = [list(range(i, size, 2)) for i in range(2)]
    parts = lax.all_to_all(sums, "ctx", 0, 0, axis_index_groups=sides)
    if replicas == 1:
        loss, passed = pl.pallas_call(
            final_kernel,
            out_shape=[pltpu.HBM((1, ndoc), F32), pltpu.HBM(passed.shape, passed.dtype)],
            in_specs=[VMEM] * 3,
            out_specs=[HBM, HBM],
            scratch_shapes=[
                pltpu.VMEM((1, ndoc), F32), pltpu.SemaphoreType.DMA((8,)), pltpu.SemaphoreType.DMA
            ],
            compiler_params=pltpu.CompilerParams(vmem_limit_bytes=40 << 20),
            name="final",
        )(parts, pos, passed)
    else:
        mine = unit(jnp.sum(parts.astype(F32), axis=0))
        cands = lax.all_gather(mine.astype(BF16), "dp", axis=0, tiled=True).astype(F32)
        loss = losses(dot(cands, mine, NT, HIGHEST) / 0.05, lax.axis_index("dp") * ndoc, pos)
    return (passed.reshape(1, 1, length, width), loss.reshape(1, 1, ndoc))


def solution(mesh):
    rows = P(("groups", "pipe"), "dp", "ctx", None)
    tokens = P(("groups", "pipe"), "dp", None, "ctx")
    docs = P(("groups", "pipe"), "dp", None)
    in_specs = (
        rows, rows, rows, tokens, tokens, P(("groups", "pipe"), "dp", "ctx"), docs, P("pipe", None)
    )
    return jax.shard_map(
        on_device, mesh=mesh, in_specs=in_specs, out_specs=(rows, docs), check_vma=False
    )
```

```python
import functools

import jax
import jax.numpy as jnp
from jax import lax
from jax.experimental import pallas as pl
from jax.experimental.pallas import tpu as pltpu
from jax.sharding import PartitionSpec as P

F32, BF16 = jnp.float32, jnp.bfloat16
HIGHEST = lax.Precision.HIGHEST
NEG = -1e30
SUB = 128
META = 16

NN = (((1,), (0,)), ((), ()))
NT = (((1,), (1,)), ((), ()))
TN = (((0,), (0,)), ((), ()))


def dot(a, b, dims=NN, precision=None):
    return lax.dot_general(a, b, dims, precision=precision, preferred_element_type=F32)


def dot1(a, b, dims=NN):
    return dot(a.astype(BF16), b.astype(BF16), dims)


def split(x):
    high = x.astype(BF16)
    return high, (x - high.astype(F32)).astype(BF16)


def dot3(a, b, dims=NN):
    (ah, al), (bh, bl) = split(a), split(b)
    return dot(ah, bh, dims) + (dot(al, bh, dims) + dot(ah, bl, dims))


def dot2(a, b):
    high, low = split(b)
    return dot(a, high) + dot(a, low)


def unit(x):
    return x * lax.rsqrt(jnp.sum(x * x, axis=-1, keepdims=True) + 1e-06)


def iotas():
    shape = (SUB, SUB)
    return lax.broadcasted_iota(jnp.int32, shape, 0), lax.broadcasted_iota(jnp.int32, shape, 1)


def per_token(rows, heads, subs):
    return jnp.concatenate([rows[:, j * SUB : (j + 1) * SUB] for j in range(subs)], axis=0)


class Decay:
    def __init__(self, gates, ids, heads, subs):
        r, c = iotas()
        upto = (c <= r).astype(F32)
        logs = per_token(jnp.log(gates), heads, subs)
        self.row = dot(logs, upto, NT, HIGHEST)
        self.col = dot(upto, logs, NT, HIGHEST)
        ids = ids.astype(F32)
        self.eye = (r == c).astype(F32)
        self.id_row = [ids[:, j * SUB : (j + 1) * SUB] for j in range(subs)]
        stacked = jnp.concatenate([jnp.broadcast_to(x, (8, SUB)) for x in self.id_row], axis=0)
        turned = dot1(self.eye, stacked, NT)
        self.id_col = [turned[:, 8 * j : 8 * j + 1] for j in range(subs)]
        self.heads, self.r, self.c = heads, r, c
        lead, tail = [], []
        for j in range(subs):
            row, last = self.row[j * heads : (j + 1) * heads], self.id_row[j][:, SUB - 1 :]
            entry = self.id_row[0][:, :1] if j == 0 else self.id_row[j - 1][:, SUB - 1 :]
            lead.append(jnp.where(self.id_row[j] == entry, jnp.exp(row), 0.0))
            tail.append(jnp.exp(jnp.where(self.id_row[j] == last, row[:, SUB - 1 :] - row, NEG)))
        self.lead = jnp.concatenate(lead, axis=0)
        self.tail = jnp.concatenate(tail, axis=0)
        self.same = [(x == y) & (r >= c) for x, y in zip(self.id_col, self.id_row)]

    def inner(self, h, j, keep):
        i = j * self.heads + h
        return jnp.exp(jnp.where(keep[j], self.col[:, i : i + 1] - self.row[i : i + 1, :], NEG))


def block(ref, h, j):
    return ref[j * SUB : (j + 1) * SUB, h * SUB : (h + 1) * SUB]


def chunk_kernel(
    heads, subs, core_ref, k_hbm, v_hbm, beta_hbm, gates_hbm, ids_hbm,
    send_ref, keep_ref, wv_ref, yy_ref, p0_ref, u0_ref, k_ref, v_ref,
    beta_ref, gates_ref, ids_ref, sems,
):
    small = [(gates_hbm, gates_ref), (ids_hbm, ids_ref), (beta_hbm, beta_ref)]
    parts = [pl.ds(j * SUB, SUB) for j in range(subs)]
    large = [(x.at[p, :], y.at[p, :]) for x, y in ((k_hbm, k_ref), (v_hbm, v_ref)) for p in parts]
    copies = [pltpu.make_async_copy(x, y, sems.at[i]) for i, (x, y) in enumerate(small + large)]
    for copy in copies:
        copy.start()
    for copy in copies[:3]:
        copy.wait()
    decay = Decay(gates_ref[...], ids_ref[...], heads, subs)
    r, c, eye = decay.r, decay.c, decay.eye
    beta = per_token(beta_ref[...], heads, subs)
    tails = decay.tail * beta
    strict = [x & (r > c) for x in decay.same]
    chains = [(h, j) for j in range(subs) for h in range(heads)]
    kn, kt, low, inv = {}, {}, {}, {}
    for h, j in chains:
        if h == 0:
            copies[3 + j].wait()
        unit_keys = unit(block(k_ref, h, j).astype(F32))
        kn[h, j] = unit_keys.astype(BF16)
        kt[h, j] = unit_keys.T
    near = ((r // 2) == (c // 2)) & (r > c)
    for h, j in chains:
        i = j * heads + h
        gram = dot(kn[h, j], kt[h, j].astype(BF16))
        full = decay.inner(h, j, strict) * gram * beta[i : i + 1, :]
        inv[h, j] = eye - jnp.where(near, full, 0.0)
        low[h, j] = full.astype(BF16)
    size = 2
    while size < SUB:
        pick = (((r // size) % 2 == 1) & ((c // size) == (r // size) - 1)).astype(BF16)
        odd = range(size, SUB, 2 * size)
        half, rows = {}, {}
        for key in chains:
            rows[key] = inv[key]
            if size >= 8:
                rows[key] = jnp.concatenate([inv[key][o : o + size] for o in odd], axis=0)
            half[key] = dot1(rows[key], low[key] * pick)
        for key in chains:
            new = rows[key] - dot1(half[key], inv[key])
            if size >= 8:
                parts = []
                for n, o in enumerate(odd):
                    parts += [inv[key][o - size : o], new[n * size : (n + 1) * size]]
                new = jnp.concatenate(parts, axis=0)
            inv[key] = new
        size *= 2
    for copy in copies[3 + subs :]:
        copy.wait()
    wv, yy, pp, uu = {}, {}, {}, {}
    for h, j in chains:
        i = j * heads + h
        xh, xl = split(inv[h, j])
        values = block(v_ref, h, j)
        wv[h, j] = dot(xh, values) + dot(xl, values)
        yy[h, j] = dot((inv[h, j] * decay.lead[i : i + 1, :]).astype(BF16), kn[h, j]).astype(BF16)
        wv_ref[j * SUB : (j + 1) * SUB, h * SUB : (h + 1) * SUB] = wv[h, j]
        yy_ref[j * SUB : (j + 1) * SUB, h * SUB : (h + 1) * SUB] = yy[h, j]
    for h, j in chains:
        i = j * heads + h
        dh, dl = split(kt[h, j] * tails[i : i + 1, :])
        wh, wl = split(wv[h, j])
        got = dot(dh, jnp.concatenate([wh, yy[h, j]], axis=1))
        pp[h, j] = decay.lead[i : i + 1, SUB - 1 :] * eye - got[:, SUB:]
        uu[h, j] = got[:, :SUB] + (dot(dl, wh) + dot(dh, wl))
    for h in range(heads):
        p0_ref[h * SUB : (h + 1) * SUB, :] = pp[h, 0]
        u0_ref[h * SUB : (h + 1) * SUB, :] = uu[h, 0]
    for j in range(1, subs):
        for h in range(heads):
            got = dot2(pp[h, j].astype(BF16), jnp.concatenate([uu[h, 0], pp[h, 0]], axis=1))
            uu[h, 0] = uu[h, j] + got[:, :SUB]
            pp[h, 0] = got[:, SUB:]
    half_heads = heads // 2
    first = core_ref[0] == 0
    for h in range(half_heads):
        for base, part in ((0, pp), (half_heads, uu)):
            lo, hi = part[h, 0].astype(BF16), part[half_heads + h, 0].astype(BF16)
            at = slice((base + h) * SUB, (base + h + 1) * SUB)
            send_ref[at, :] = jnp.where(first, hi, lo)
            keep_ref[at, :] = jnp.where(first, lo, hi)
    start = decay.id_row[0][:, :1]
    end = decay.id_row[-1][:, SUB - 1 :]
    which = lax.broadcasted_iota(jnp.int32, (META, SUB), 0) < META // 2
    meta = jnp.where(which, end, start).astype(BF16)
    send_ref[heads * SUB :, :] = meta
    keep_ref[heads * SUB :, :] = meta


def query_kernel(
    heads, subs, q_ref, k_ref, beta_ref, gates_ref, ids_ref, wv_ref, yy_ref, p0_ref, u0_ref,
    gain_in, pos_in, local_ref, reach_ref, gain_ref, pos_ref,
):
    gain_ref[...] = gain_in[...]
    pos_ref[...] = pos_in[...]
    decay = Decay(gates_ref[...], ids_ref[...], heads, subs)
    beta = per_token(beta_ref[...], heads, subs)
    lead = dot(decay.eye, decay.lead, NT, HIGHEST)
    chains = [(h, j) for j in range(subs) for h in range(heads)]
    qn, attend, reach, local = {}, {}, {}, {}
    for h, j in chains:
        i = j * heads + h
        qn[h, j] = unit(block(q_ref, h, j).astype(F32))
        kn = unit(block(k_ref, h, j).astype(F32))
        attend[h, j] = decay.inner(h, j, decay.same) * dot3(qn[h, j], kn, NT) * beta[i : i + 1, :]
    for h, j in chains:
        i = j * heads + h
        ah, al = split(attend[h, j])
        wh, wl = split(block(wv_ref, h, j))
        reach[h, j] = lead[:, i : i + 1] * qn[h, j] - dot(ah, block(yy_ref, h, j))
        local[h, j] = dot(ah, wh) + (dot(al, wh) + dot(ah, wl))
    for h, j in chains:
        if j > 0:
            at = slice(h * SUB, (h + 1) * SUB)
            got = dot3(reach[h, j], jnp.concatenate([u0_ref[at, :], p0_ref[at, :]], axis=1))
            local[h, j] = local[h, j] + got[:, :SUB]
            reach[h, j] = got[:, SUB:]
    for h, j in chains:
        rows, cols = slice(j * SUB, (j + 1) * SUB), slice(h * SUB, (h + 1) * SUB)
        local_ref[rows, cols] = local[h, j]
        reach_ref[rows, 2 * h * SUB : 2 * (h + 1) * SUB] = jnp.concatenate(split(reach[h, j]), axis=1)


def ends(ref, rows):
    meta = ref[rows : rows + META, :].astype(F32)
    return meta[META // 2 : META // 2 + 1, :], meta[:1, :]


def pair_kernel(heads, core_ref, keep_ref, got_ref, full_ref, tail_ref):
    half = heads // 2
    first = core_ref[0] == 0
    own, other = ends(keep_ref, heads * SUB), ends(got_ref, heads * SUB)
    early = [jnp.where(first, a, b) for a, b in zip(own, other)]
    late = [jnp.where(first, b, a) for a, b in zip(own, other)]
    joined = (early[1] == late[0]).astype(F32)
    for h in range(half):
        at, up = slice(h * SUB, (h + 1) * SUB), slice((half + h) * SUB, (half + h + 1) * SUB)
        p1 = jnp.where(first, keep_ref[at, :], got_ref[at, :])
        p2 = jnp.where(first, got_ref[at, :], keep_ref[at, :])
        u1 = jnp.where(first, keep_ref[up, :], got_ref[up, :])
        u2 = jnp.where(first, got_ref[up, :], keep_ref[up, :])
        full_ref[at, :] = (joined * dot(p2, p1)).astype(BF16)
        state = (u2.astype(F32) + joined * dot(p2, u1)).astype(BF16)
        full_ref[up, :] = state
        tail_ref[at, :] = state
    which = lax.broadcasted_iota(jnp.int32, (META, SUB), 0) < META // 2
    meta = jnp.where(which, late[1], early[0]).astype(BF16)
    full_ref[heads * SUB :, :] = meta
    tail_ref[half * SUB :, :] = meta


def enter_kernel(heads, reach, core_ref, keep_ref, got_ref, *refs):
    chips, (send_ref, mine_ref) = refs[:reach], refs[reach:]
    half = heads // 2
    first = core_ref[0] == 0
    own, other = ends(keep_ref, heads * SUB), ends(got_ref, heads * SUB)
    early = [jnp.where(first, a, b) for a, b in zip(own, other)]
    late = [jnp.where(first, b, a) for a, b in zip(own, other)]
    marks = [(early[0], None)]
    for d, ref in enumerate(chips):
        marks.append(ends(ref, (heads if d < reach - 1 else half) * SUB))
    links = [(marks[d][0] == marks[d + 1][1]).astype(F32) for d in range(reach)]
    joined = (early[1] == late[0]).astype(F32)
    ats = [slice(h * SUB, (h + 1) * SUB) for h in range(half)]
    ups = [slice((half + h) * SUB, (half + h + 1) * SUB) for h in range(half)]
    states = [chips[-1][at, :].astype(F32) for at in ats]
    for d in range(reach - 2, -1, -1):
        moved = [dot2(chips[d][at, :], state) for at, state in zip(ats, states)]
        states = [chips[d][up, :].astype(F32) + links[d + 1] * x for up, x in zip(ups, moved)]
    states = [links[0] * state for state in states]
    moved = [
        dot2(jnp.where(first, keep_ref[at, :], got_ref[at, :]), state) for at, state in zip(ats, states)
    ]
    for at, up, state, x in zip(ats, ups, states, moved):
        u1 = jnp.where(first, keep_ref[up, :], got_ref[up, :])
        middle = joined * (u1.astype(F32) + x)
        send_ref[at, :] = jnp.where(first, middle, state)
        mine_ref[at, :] = jnp.where(first, state, middle)


def rows_kernel(
    heads, ndoc, own, core_ref, state_ref, local_ref, reach_ref, v_ref, gain_ref, ids_ref, *refs
):
    out_ref, pooled_ref = refs[-2:]
    half = heads // 2
    group = core_ref[0] if own else 1 - core_ref[0]
    docs = lax.broadcasted_iota(jnp.int32, (ndoc, v_ref.shape[0]), 0)
    onehot = (docs == ids_ref[...]).astype(F32).astype(BF16)
    gain = gain_ref[...]
    mean = jnp.full((SUB, SUB), 1.0 / SUB, BF16)
    cols = [pl.ds(pl.multiple_of((group * half + h) * SUB, SUB), SUB) for h in range(half)]
    outs = []
    for h, x in enumerate(cols):
        high, low = split(state_ref[h * SUB : (h + 1) * SUB, :])
        wide = pl.ds(pl.multiple_of((group * half + h) * 2 * SUB, 2 * SUB), 2 * SUB)
        near = reach_ref[:, wide]
        moved = dot(near, jnp.concatenate([high, high], axis=0)) + dot(near[:, :SUB], low)
        outs.append(local_ref[:, x] + moved)
    scales = [lax.rsqrt(dot1(o * o, mean) + 1e-06) * gain for o in outs]
    outs = [
        (v_ref[:, x].astype(F32) + o * scale).astype(BF16) for x, o, scale in zip(cols, outs, scales)
    ]
    sums = [dot(onehot, out).astype(BF16) for out in outs]
    for x, out, pooled in zip(cols, outs, sums):
        out_ref[:, x] = out
        pooled_ref[:, x] = pooled


def losses(scores, own, pos):
    cidx = lax.broadcasted_iota(jnp.int32, scores.shape, 0)
    didx = lax.broadcasted_iota(jnp.int32, scores.shape, 1)
    total = jnp.sum(jnp.where(cidx != own + didx, jnp.exp(scores), 0.0), axis=0, keepdims=True)
    picked = jnp.sum(jnp.where(cidx == pos, scores, 0.0), axis=0, keepdims=True)
    return jnp.log(total) - picked


def add_kernel(a_ref, b_ref, out_ref):
    total = (a_ref[...].astype(F32) + b_ref[...].astype(F32)).astype(BF16)
    for i in range(out_ref.shape[0]):
        out_ref[i] = total


def store_rows(rows_ref, out_ref, sems):
    pieces = sems.shape[0]
    step = rows_ref.shape[0] // pieces
    at = [pl.ds(i * step, step) for i in range(pieces)]
    return [pltpu.make_async_copy(rows_ref.at[x, :], out_ref.at[x, :], sems.at[i]) for i, x in enumerate(at)]


def final_kernel(parts_ref, pos_ref, rows_ref, loss_out, out_ref, loss_ref, sems, loss_sem):
    copies = store_rows(rows_ref, out_ref, sems)
    for copy in copies:
        copy.start()
    sums = jnp.sum(parts_ref[...].astype(F32), axis=0)
    gram = dot(sums, sums, NT, HIGHEST)
    cidx = lax.broadcasted_iota(jnp.int32, gram.shape, 0)
    didx = lax.broadcasted_iota(jnp.int32, gram.shape, 1)
    squares = jnp.where(cidx == didx, gram, 0.0)
    across = lax.rsqrt(jnp.sum(squares, axis=0, keepdims=True) + 1e-06)
    down = lax.rsqrt(jnp.sum(squares, axis=1, keepdims=True) + 1e-06)
    loss_ref[...] = losses(gram * across * down / 0.05, 0, pos_ref[...])
    copies.append(pltpu.make_async_copy(loss_ref, loss_out, loss_sem))
    copies[-1].start()
    for copy in copies:
        copy.wait()


VMEM = pl.BlockSpec(memory_space=pltpu.VMEM)
SMEM = pl.BlockSpec(memory_space=pltpu.SMEM)
HBM = pl.BlockSpec(memory_space=pltpu.HBM)


def call(body, outs, name, specs, flops=0, scratch=(), aliases={}):
    return pl.pallas_call(
        body,
        out_shape=[jax.ShapeDtypeStruct(s, d) for s, d in outs],
        in_specs=specs,
        out_specs=[VMEM] * len(outs),
        scratch_shapes=scratch,
        input_output_aliases=aliases,
        compiler_params=pltpu.CompilerParams(vmem_limit_bytes=40 << 20),
        cost_estimate=pl.CostEstimate(flops=flops, bytes_accessed=4 << 20, transcendentals=0),
        name=name,
    )


def on_device(rows_in, queries, keys, strengths, gates, doc_ids, positives, norm_gain):
    length, width = rows_in.shape[2], rows_in.shape[3]
    heads, ndoc = strengths.shape[2], positives.shape[2]
    subs = length // SUB
    half = heads // 2
    size, pipes, replicas = (lax.axis_size(x) for x in ("ctx", "pipe", "dp"))
    chips = size // 2
    reach = chips // 4
    v, q, k = rows_in[0, 0], queries[0, 0], keys[0, 0]
    beta, gate, ids = strengths[0, 0], gates[0, 0], doc_ids[0]
    core = (lax.axis_index("ctx") % 2).astype(jnp.int32).reshape(1)

    def swapped(x):
        return lax.ppermute(x, "ctx", [(i, i ^ 1) for i in range(size)])

    def from_behind(x, d):
        return lax.ppermute(x, "ctx", [(i, i + 2 * d) for i in range(size - 2 * d)])

    big = (heads * SUB + META, SUB)
    send, keep, wv, yy, p0, u0, k, v, beta, gate, ids = call(
        functools.partial(chunk_kernel, heads, subs),
        [(big, BF16), (big, BF16), ((length, width), F32), ((length, width), BF16)]
        + [((heads * SUB, SUB), F32)] * 2 + [((length, width), BF16)] * 2
        + [((heads, length), F32)] * 2 + [((1, length), jnp.int32)],
        "chunks", [SMEM] + [HBM] * 5, 1 << 31,
        [pltpu.SemaphoreType.DMA((3 + 2 * subs,))],
    )(core, *(pltpu.with_memory_space_constraint(x, pltpu.HBM) for x in (k, v, beta, gate, ids)))
    got = swapped(send)
    full, tail = call(
        functools.partial(pair_kernel, heads),
        [(big, BF16), ((half * SUB + META, SUB), BF16)],
        "pair", [SMEM, VMEM, VMEM], 1 << 25,
    )(core, keep, got)
    arrived = [from_behind(full, d) for d in range(1, reach)] + [from_behind(tail, reach)]
    local, reached, gain, pos = call(
        functools.partial(query_kernel, heads, subs),
        [((length, width), F32), ((length, 2 * width), BF16), (norm_gain.shape, F32), ((1, ndoc), jnp.int32)],
        "queries", [VMEM] * 11, 1 << 31,
    )(q, k, beta, gate, ids, wv, yy, p0, u0, norm_gain, positives[0])
    arrived, local, reached, gain, pos = lax.optimization_barrier((arrived, local, reached, gain, pos))
    give, mine = call(
        functools.partial(enter_kernel, heads, reach),
        [((half * SUB, SUB), F32)] * 2,
        "enter", [SMEM] + [VMEM] * (2 + reach), 1 << 25,
    )(core, keep, got, *arrived)
    theirs = swapped(give)
    outs = [((length, width), BF16), ((ndoc, width), BF16)]
    rest = (local, reached, v, gain, ids)
    begun = call(
        functools.partial(rows_kernel, heads, ndoc, True), outs, "rows_own", [SMEM] + [VMEM] * 6, 1 << 31
    )(core, mine, *rest)
    rows_out, pooled = call(
        functools.partial(rows_kernel, heads, ndoc, False), outs, "rows_other",
        [SMEM] + [VMEM] * 8, 1 << 26, aliases={7: 0, 8: 1},
    )(core, theirs, *rest, *begun)
    passed = lax.ppermute(rows_out, "pipe", [(i, (i + 1) % pipes) for i in range(pipes)])
    (sums,) = call(add_kernel, [((chips, ndoc, width), BF16)], "sums", [VMEM, VMEM])(pooled, swapped(pooled))
    sides = [list(range(i, size, 2)) for i in range(2)]
    parts = lax.all_to_all(sums, "ctx", 0, 0, axis_index_groups=sides)
    if replicas == 1:
        loss, passed = pl.pallas_call(
            final_kernel,
            out_shape=[pltpu.HBM((1, ndoc), F32), pltpu.HBM(passed.shape, passed.dtype)],
            in_specs=[VMEM] * 3,
            out_specs=[HBM, HBM],
            scratch_shapes=[
                pltpu.VMEM((1, ndoc), F32), pltpu.SemaphoreType.DMA((8,)), pltpu.SemaphoreType.DMA
            ],
            compiler_params=pltpu.CompilerParams(vmem_limit_bytes=40 << 20),
            name="final",
        )(parts, pos, passed)
    else:
        mine = unit(jnp.sum(parts.astype(F32), axis=0))
        cands = lax.all_gather(mine.astype(BF16), "dp", axis=0, tiled=True).astype(F32)
        loss = losses(dot(cands, mine, NT, HIGHEST) / 0.05, lax.axis_index("dp") * ndoc, pos)
    return (passed.reshape(1, 1, length, width), loss.reshape(1, 1, ndoc))


def solution(mesh):
    rows = P(("groups", "pipe"), "dp", "ctx", None)
    tokens = P(("groups", "pipe"), "dp", None, "ctx")
    docs = P(("groups", "pipe"), "dp", None)
    in_specs = (
        rows, rows, rows, tokens, tokens, P(("groups", "pipe"), "dp", "ctx"), docs, P("pipe", None)
    )
    return jax.shard_map(
        on_device, mesh=mesh, in_specs=in_specs, out_specs=(rows, docs), check_vma=False
    )
```
